128 devices in a mesh: obs: 8 (over z_hi, y), unk: 16 (over z_lo, x, core).
Axes of the slice: x: 4, y: 4, z: 4 (z_hi: 2, z_lo: 2; z = z_hi * 2 + z_lo), core: 2. Of those that a mesh axis runs over, the one named last changes fastest.
Arguments:
- design: float32 [8192, 24576], P('obs', 'unk'), may hold values from -0.0625 to 0.0625
- weights: float32 [8192], P('obs'), may hold values from 0.25 to 4
Outputs:
- factor: float32 [24576, 1024], P(('unk', 'obs'))
The draws below stay inside these ranges and needn't reach their ends.
All inputs are finite; a program needn't handle non-finite values.
Results may differ from the reference program's by a relative error of at most 0.00011.
Values sent between devices are 32-bit elements; how exact they have to be, the bound alone decides.
No kernel may reach another device: no remote copies, remote signals or barrier semaphores. Data moves between devices by JAX's collectives and lax.ppermute only.
A program may use at most 128 MiB of HBM per device.

```python
import math
import jax
import jax.numpy as jnp
from jax import lax

N = 24576
PANEL = 512
M = 8192


def steps_of(own_key, shape, cuts, least, top_value):
    loudness, own = 1.0, jax.random.fold_in(own_key, 6)
    for position, shards_of in cuts:
        draws = jnp.exp(jax.random.uniform(jax.random.fold_in(own, position), (shards_of,), jnp.float32, least / len(cuts), top_value / len(cuts)))
        loudness = loudness * jnp.repeat(draws, shape[position] // shards_of).reshape([-1 if axis == position else 1 for axis in range(len(shape))])
    return loudness


def noise(own_key, shape, scale, most, cuts=(), held_as=jnp.bfloat16):
    loudness = steps_of(own_key, shape, cuts, -0.22, 0.18) if cuts else 1.0
    values = jax.random.normal(own_key, shape, jnp.float32) * scale * loudness
    return jnp.minimum(jnp.maximum(values, -most), most).astype(held_as)


def setup_inputs(seed: int = 0) -> dict:
    key_list = jax.random.split(jax.random.key(seed), 3)
    return {
        "design": noise(key_list[0], (M, N), M ** -0.5, 0.0625, ((0, 8), (1, 16)), jnp.float32),
        "weights": jnp.clip(jnp.exp(math.log(4.0) - 2.7725887 * jax.random.uniform(key_list[1], (M,), jnp.float32) ** steps_of(key_list[1], (M,), ((0, 8),), -0.2, 0.2)), 0.25, 4.0),
    }


def reference(design, weights):
    panel_cols = design[:, :2 * PANEL]
    weighted = panel_cols * weights[:, None]
    gram = lax.dot_general(design.astype(jnp.float32), weighted.astype(jnp.float32), (((0,), (0,)), ((), ())), precision=lax.Precision.HIGHEST, preferred_element_type=jnp.float32)
    top_block = gram[:2 * PANEL]
    diag_factor = jnp.linalg.cholesky(top_block)
    return lax.linalg.triangular_solve(diag_factor, gram, left_side=False, lower=True, transpose_a=True)
```

```python
import jax, jax.numpy as jnp
from jax import lax
from jax.experimental import pallas as pl
from jax.experimental.pallas import tpu as pltpu
from jax.sharding import PartitionSpec as P

BLOCK = 128
SUB = 8
HALF = BLOCK // 2


def rep(row):
    return jnp.broadcast_to(row, (SUB, BLOCK))


def split(x):
    hi = x.astype(jnp.bfloat16)
    return hi, (x - hi.astype(jnp.float32)).astype(jnp.bfloat16)


def dot_t(a, b):
    return lax.dot_general(a, b, (((1,), (1,)), ((), ())), preferred_element_type=jnp.float32)


def dot3_t(a, b):
    (ah, al), (bh, bl) = a, b
    return dot_t(ah, bh) + (dot_t(ah, bl) + dot_t(al, bh))


def invert_diag(block_ref, inv_ref):
    lane = lax.broadcasted_iota(jnp.int32, (SUB, BLOCK), 1)
    sub = lax.broadcasted_iota(jnp.int32, (SUB, BLOCK), 0)
    panels = BLOCK // SUB
    groups = []
    for q in range(panels):
        groups.append(block_ref[q * SUB : (q + 1) * SUB, :])
    carried = None
    for p in range(panels):
        r0 = p * SUB
        w = [rep(groups[p][i : i + 1, :]) for i in range(SUB)]
        e = {}
        for i in range(SUB):
            for c in range(i, SUB):
                e[i, c] = rep(w[i][:, r0 + c : r0 + c + 1])
        if carried is not None:
            a = [[rep(carried[k][:, r0 + i : r0 + i + 1]) for i in range(SUB)] for k in range(SUB)]
            passed = (lane >= r0 - SUB) & (lane < r0)
            w = [jnp.where(passed, 0.0, row) for row in w]
            for k in range(SUB):
                for i in range(SUB):
                    w[i] = w[i] - a[k][i] * carried[k]
                    for c in range(i, SUB):
                        e[i, c] = e[i, c] - a[k][i] * a[k][c]
        inside = (lane >= r0) & (lane < r0 + SUB)
        for i in range(SUB):
            w[i] = jnp.where(inside, jnp.where(lane == r0 + i, 1.0, 0.0), w[i])
        for c in range(SUB):
            inv = lax.rsqrt(e[c, c])
            w[c] = w[c] * inv
            u = {i: e[c, i] * inv for i in range(c + 1, SUB)}
            for i in range(c + 1, SUB):
                w[i] = w[i] - u[i] * w[c]
                for j in range(i, SUB):
                    e[i, j] = e[i, j] - u[i] * u[j]
        natural = w[0]
        for i in range(1, SUB):
            natural = jnp.where(sub == i, w[i], natural)
        inv_ref[r0 : r0 + SUB, :] = jnp.where(lane < r0 + SUB, natural, 0.0)
        if p + 2 < panels:
            turned = natural.T
            for q in range(p + 2, panels):
                columns = turned[q * SUB : (q + 1) * SUB, :]
                groups[q] = jnp.where(inside, 0.0, groups[q])
                for k in range(SUB):
                    groups[q] = groups[q] - jnp.broadcast_to(columns[:, k : k + 1], (SUB, BLOCK)) * w[k]
        carried = w


def unpack(where_ref, mine_ref, other_ref, work, pieces):
    count, quarter, _ = mine_ref.shape
    obs, core = where_ref[0], where_ref[1]
    own = pl.ds(pl.multiple_of(core * quarter, quarter), quarter)
    others = pl.ds(pl.multiple_of((1 - core) * quarter, quarter), quarter)
    for k in range(count):
        pieces[obs ^ k, own, :] = mine_ref[k]
        pieces[obs ^ k, others, :] = other_ref[k]
    for t in range(count):
        low, high = t, 2 * count - 1 - t
        cut, rest = (low // 2 + 1) * BLOCK, (high // 2 + 1) * BLOCK
        work[low * HALF : (low + 1) * HALF, :cut] = pieces[t, :, :cut]
        work[high * HALF : (high + 1) * HALF, :rest] = pieces[t, :, cut:]


def chol_kernel(where_ref, mine_ref, other_ref, low_ref, inv_ref, work, pieces, diag, dinv, hi_ref, lo_ref):
    width = work.shape[0]
    blocks = width // BLOCK
    work[...] = jnp.zeros_like(work)
    unpack(where_ref, mine_ref, other_ref, work, pieces)

    def step(k, _):
        at = pl.multiple_of(k * BLOCK, BLOCK)
        diag[...] = work[pl.ds(at, BLOCK), pl.ds(at, BLOCK)]
        invert_diag(diag, dinv)
        inverse = dinv[...]
        inv_ref[pl.ds(at, BLOCK), :] = inverse
        inverse = split(inverse)
        hi_ref[...] = jnp.zeros_like(hi_ref)
        lo_ref[...] = jnp.zeros_like(lo_ref)

        def below(i, _):
            rows = pl.ds(pl.multiple_of(i * BLOCK, BLOCK), BLOCK)
            new = dot3_t(split(work[rows, pl.ds(at, BLOCK)]), inverse)
            low_ref[rows, pl.ds(at, BLOCK)] = new
            hi, lo = split(new)
            hi_ref[rows, :] = hi
            lo_ref[rows, :] = lo
            return 0

        lax.fori_loop(k + 1, blocks, below, 0)

        def trail(i, _):
            rows = pl.ds(pl.multiple_of(i * BLOCK, BLOCK), BLOCK)
            work[rows, :] = work[rows, :] - dot3_t(
                (hi_ref[rows, :], lo_ref[rows, :]), (hi_ref[...], lo_ref[...])
            )
            return 0

        lax.fori_loop(k + 1, blocks, trail, 0)
        return 0

    lax.fori_loop(0, blocks, step, 0)


def cholesky_parts(where, mine, other):
    count, quarter, packed = mine.shape
    width = count * BLOCK
    vmem = pl.BlockSpec(memory_space=pltpu.VMEM)
    return pl.pallas_call(
        chol_kernel,
        out_shape=(
            jax.ShapeDtypeStruct((width, width), jnp.float32),
            jax.ShapeDtypeStruct((width, BLOCK), jnp.float32),
        ),
        in_specs=[pl.BlockSpec(memory_space=pltpu.SMEM), vmem, vmem],
        out_specs=(vmem, vmem),
        scratch_shapes=[
            pltpu.VMEM((width, width), jnp.float32),
            pltpu.VMEM((count, 2 * quarter, packed), jnp.float32),
            pltpu.VMEM((BLOCK, BLOCK), jnp.float32),
            pltpu.VMEM((BLOCK, BLOCK), jnp.float32),
            pltpu.VMEM((width, BLOCK), jnp.bfloat16),
            pltpu.VMEM((width, BLOCK), jnp.bfloat16),
        ],
        compiler_params=pltpu.CompilerParams(vmem_limit_bytes=32 << 20),
        cost_estimate=pl.CostEstimate(flops=80_000_000_000, bytes_accessed=8 << 20, transcendentals=0),
    )(where, mine, other)


def solve_kernel(gram_ref, low_ref, inv_ref, out_ref):
    rows, width = gram_ref.shape
    blocks = width // BLOCK
    out_ref[...] = gram_ref[...]
    for k in range(blocks):
        cols = slice(k * BLOCK, (k + 1) * BLOCK)
        new = dot3_t(split(out_ref[:, cols]), split(inv_ref[cols, :]))
        out_ref[:, cols] = new
        if k + 1 < blocks:
            rest = slice((k + 1) * BLOCK, width)
            out_ref[:, rest] = out_ref[:, rest] - dot3_t(split(new), split(low_ref[rest, cols]))


def solve_rows(gram, low, inv):
    return pl.pallas_call(
        solve_kernel,
        out_shape=jax.ShapeDtypeStruct(gram.shape, jnp.float32),
        in_specs=[pl.BlockSpec(memory_space=pltpu.VMEM)] * 3,
        out_specs=pl.BlockSpec(memory_space=pltpu.VMEM),
        compiler_params=pltpu.CompilerParams(vmem_limit_bytes=24 << 20),
    )(gram, low, inv)

BOTH = ("obs", "unk")
OBS, UNK = 8, 16
WIDTH = 1024


def add_all(parts):
    total = parts[0]
    for part in parts[1:]:
        total = total + part
    return total


def from_first(slices, unk):
    got = [jnp.where(unk == 0, slices[0], 0.0)]
    for u in range(1, UNK):
        pairs = [(o * UNK, o * UNK + u) for o in range(OBS)]
        got.append(lax.ppermute(slices[u], BOTH, pairs))
    return add_all(got)


def over_obs(pick, units=range(UNK)):
    got = []
    for k in range(1, OBS):
        pairs = [(o * UNK + u, (o ^ k) * UNK + u) for o in range(OBS) for u in units]
        got.append(lax.ppermute(pick(k), BOTH, pairs))
    return got


def high_dot(left, right):
    return lax.dot_general(
        left, right, (((0,), (0,)), ((), ())),
        precision=lax.Precision.HIGH, preferred_element_type=jnp.float32,
    )


def pack(top):
    pieces = []
    for t in range(OBS):
        low, high = t, 2 * OBS - 1 - t
        pieces.append(jnp.concatenate([
            top[low * HALF : (low + 1) * HALF, : (low // 2 + 1) * BLOCK],
            top[high * HALF : (high + 1) * HALF, : (high // 2 + 1) * BLOCK],
        ], axis=1))
    return jnp.stack(pieces)


def local(design, weights):
    obs, unk = lax.axis_index("obs"), lax.axis_index("unk")
    chip, core = unk // 2, unk % 2
    head = design[:, :WIDTH]
    weighted = head * weights[:, None]

    pieces = pack(high_dot(head, weighted))
    piece_of = lambda k: lax.dynamic_index_in_dim(pieces, obs ^ k, 0, keepdims=False)
    summed = add_all([piece_of(0)] + over_obs(piece_of, (0,)))
    quarter = HALF // 2
    halves = [summed[c * quarter : (c + 1) * quarter] for c in range(2)]
    part = from_first([halves[u % 2] for u in range(UNK)], unk)
    mine_top = jnp.stack([part] + over_obs(lambda k: part))
    swap = [(u, u ^ 1) for u in range(UNK)]
    other_top = lax.ppermute(mine_top, "unk", swap)

    rows = weighted.shape[0] // 2
    slices = [weighted[(u % 2) * rows : (u % 2 + 1) * rows, (u // 2) * BLOCK : (u // 2 + 1) * BLOCK] for u in range(UNK)]
    part = from_first(slices, unk)
    mine = jnp.zeros((rows, WIDTH), jnp.float32)
    for k in range(UNK // 2):
        if k == 0:
            got = part
        else:
            got = lax.ppermute(part, "unk", [(u, u ^ (2 * k)) for u in range(UNK)])
        mine = lax.dynamic_update_slice(mine, got, (0, (chip ^ k) * BLOCK))
    other = lax.ppermute(mine, "unk", swap)
    first = lax.dynamic_slice_in_dim(design, core * rows, rows, 0)
    second = lax.dynamic_slice_in_dim(design, (1 - core) * rows, rows, 0)
    partial_value = high_dot(first, mine) + high_dot(second, other)

    owned = partial_value.shape[0] // OBS
    rows_of = lambda k: lax.dynamic_slice_in_dim(partial_value, (obs ^ k) * owned, owned, 0)
    sends = [rows_of(k) for k in range(OBS)]
    mine_top, other_top, sends = lax.optimization_barrier((mine_top, other_top, sends))
    received = over_obs(lambda k: sends[k])
    where = jnp.stack([obs, core]).astype(jnp.int32)
    low, inverse = cholesky_parts(where, mine_top, other_top)
    owned_rows = add_all([sends[0]] + received)
    return solve_rows(owned_rows, low, inverse)


def solution(mesh):
    return jax.shard_map(
        local,
        mesh=mesh,
        in_specs=(P("obs", "unk"), P("obs")),
        out_specs=P(("unk", "obs"), None),
        check_vma=False,
    )
```

```python
import jax, jax.numpy as jnp
from jax import lax
from jax.experimental import pallas as pl
from jax.experimental.pallas import tpu as pltpu
from jax.sharding import PartitionSpec as P

BLOCK = 128
SUB = 8
STRIP = 32


def rep(row):
    return jnp.broadcast_to(row, (SUB, BLOCK))


def split(x):
    hi = x.astype(jnp.bfloat16)
    return hi, (x - hi.astype(jnp.float32)).astype(jnp.bfloat16)


def dot_t(a, b):
    return lax.dot_general(a, b, (((1,), (1,)), ((), ())), preferred_element_type=jnp.float32)


def dot3_t(a, b):
    (ah, al), (bh, bl) = a, b
    return dot_t(ah, bh) + (dot_t(ah, bl) + dot_t(al, bh))


def invert_diag(block_ref, inv_ref):
    lane = lax.broadcasted_iota(jnp.int32, (SUB, BLOCK), 1)
    sub = lax.broadcasted_iota(jnp.int32, (SUB, BLOCK), 0)
    panels = BLOCK // SUB
    groups = []
    for q in range(panels):
        groups.append(block_ref[q * SUB : (q + 1) * SUB, :])
    carried = None
    for p in range(panels):
        r0 = p * SUB
        w = [rep(groups[p][i : i + 1, :]) for i in range(SUB)]
        e = {}
        for i in range(SUB):
            for c in range(i, SUB):
                e[i, c] = rep(w[i][:, r0 + c : r0 + c + 1])
        if carried is not None:
            a = [[rep(carried[k][:, r0 + i : r0 + i + 1]) for i in range(SUB)] for k in range(SUB)]
            passed = (lane >= r0 - SUB) & (lane < r0)
            w = [jnp.where(passed, 0.0, row) for row in w]
            for k in range(SUB):
                for i in range(SUB):
                    w[i] = w[i] - a[k][i] * carried[k]
                    for c in range(i, SUB):
                        e[i, c] = e[i, c] - a[k][i] * a[k][c]
        inside = (lane >= r0) & (lane < r0 + SUB)
        for i in range(SUB):
            w[i] = jnp.where(inside, jnp.where(lane == r0 + i, 1.0, 0.0), w[i])
        for c in range(SUB):
            inv = lax.rsqrt(e[c, c])
            w[c] = w[c] * inv
            u = {i: e[c, i] * inv for i in range(c + 1, SUB)}
            for i in range(c + 1, SUB):
                w[i] = w[i] - u[i] * w[c]
                for j in range(i, SUB):
                    e[i, j] = e[i, j] - u[i] * u[j]
        natural = w[0]
        for i in range(1, SUB):
            natural = jnp.where(sub == i, w[i], natural)
        inv_ref[r0 : r0 + SUB, :] = jnp.where(lane < r0 + SUB, natural, 0.0)
        if p + 2 < panels:
            turned = natural.T
            for q in range(p + 2, panels):
                columns = turned[q * SUB : (q + 1) * SUB, :]
                groups[q] = jnp.where(inside, 0.0, groups[q])
                for k in range(SUB):
                    groups[q] = groups[q] - jnp.broadcast_to(columns[:, k : k + 1], (SUB, BLOCK)) * w[k]
        carried = w


def unpack(where_ref, mine_ref, other_ref, work, pieces):
    count = mine_ref.shape[0]
    chip, core = where_ref[0], where_ref[1]
    for k in range(count):
        pieces[2 * (chip ^ k) + core] = mine_ref[k]
        pieces[2 * (chip ^ k) + 1 - core] = other_ref[k]
    for t in range(2 * count):
        low, high = t * STRIP, (4 * count - 1 - t) * STRIP
        cut, rest = (low // BLOCK + 1) * BLOCK, (high // BLOCK + 1) * BLOCK
        work[low : low + STRIP, :cut] = pieces[t, :, :cut]
        work[high : high + STRIP, :rest] = pieces[t, :, cut:]


def chol_kernel(where_ref, mine_ref, other_ref, low_ref, inv_ref, work, pieces, diag, dinv, hi_ref, lo_ref):
    width = work.shape[0]
    blocks = width // BLOCK
    work[...] = jnp.zeros_like(work)
    unpack(where_ref, mine_ref, other_ref, work, pieces)

    def step(k, _):
        at = pl.multiple_of(k * BLOCK, BLOCK)
        diag[...] = work[pl.ds(at, BLOCK), pl.ds(at, BLOCK)]
        invert_diag(diag, dinv)
        inverse = dinv[...]
        inv_ref[pl.ds(at, BLOCK), :] = inverse
        inverse = split(inverse)
        hi_ref[...] = jnp.zeros_like(hi_ref)
        lo_ref[...] = jnp.zeros_like(lo_ref)

        def below(i, _):
            rows = pl.ds(pl.multiple_of(i * BLOCK, BLOCK), BLOCK)
            new = dot3_t(split(work[rows, pl.ds(at, BLOCK)]), inverse)
            low_ref[rows, pl.ds(at, BLOCK)] = new
            hi, lo = split(new)
            hi_ref[rows, :] = hi
            lo_ref[rows, :] = lo
            return 0

        lax.fori_loop(k + 1, blocks, below, 0)

        def trail(i, _):
            rows = pl.ds(pl.multiple_of(i * BLOCK, BLOCK), BLOCK)
            work[rows, :] = work[rows, :] - dot3_t(
                (hi_ref[rows, :], lo_ref[rows, :]), (hi_ref[...], lo_ref[...])
            )
            return 0

        lax.fori_loop(k + 1, blocks, trail, 0)
        return 0

    lax.fori_loop(0, blocks, step, 0)


def cholesky_parts(where, mine, other):
    count, strip, packed = mine.shape
    width = count * BLOCK
    vmem = pl.BlockSpec(memory_space=pltpu.VMEM)
    return pl.pallas_call(
        chol_kernel,
        out_shape=(
            jax.ShapeDtypeStruct((width, width), jnp.float32),
            jax.ShapeDtypeStruct((width, BLOCK), jnp.float32),
        ),
        in_specs=[pl.BlockSpec(memory_space=pltpu.SMEM), vmem, vmem],
        out_specs=(vmem, vmem),
        scratch_shapes=[
            pltpu.VMEM((width, width), jnp.float32),
            pltpu.VMEM((2 * count, strip, packed), jnp.float32),
            pltpu.VMEM((BLOCK, BLOCK), jnp.float32),
            pltpu.VMEM((BLOCK, BLOCK), jnp.float32),
            pltpu.VMEM((width, BLOCK), jnp.bfloat16),
            pltpu.VMEM((width, BLOCK), jnp.bfloat16),
        ],
        compiler_params=pltpu.CompilerParams(vmem_limit_bytes=32 << 20),
        cost_estimate=pl.CostEstimate(flops=80_000_000_000, bytes_accessed=8 << 20, transcendentals=0),
    )(where, mine, other)


def solve_kernel(gram_ref, low_ref, inv_ref, out_ref):
    rows, width = gram_ref.shape
    blocks = width // BLOCK
    out_ref[...] = gram_ref[...]
    for k in range(blocks):
        cols = slice(k * BLOCK, (k + 1) * BLOCK)
        new = dot3_t(split(out_ref[:, cols]), split(inv_ref[cols, :]))
        out_ref[:, cols] = new
        if k + 1 < blocks:
            rest = slice((k + 1) * BLOCK, width)
            out_ref[:, rest] = out_ref[:, rest] - dot3_t(split(new), split(low_ref[rest, cols]))


def solve_rows(gram, low, inv):
    return pl.pallas_call(
        solve_kernel,
        out_shape=jax.ShapeDtypeStruct(gram.shape, jnp.float32),
        in_specs=[pl.BlockSpec(memory_space=pltpu.VMEM)] * 3,
        out_specs=pl.BlockSpec(memory_space=pltpu.VMEM),
        compiler_params=pltpu.CompilerParams(vmem_limit_bytes=24 << 20),
    )(gram, low, inv)


BOTH = ("obs", "unk")
OBS, UNK = 8, 16
CHIPS = UNK // 2
WIDTH = 1024


def add_all(parts):
    total = parts[0]
    for part in parts[1:]:
        total = total + part
    return total


def swap_cores(value):
    return lax.ppermute(value, "unk", [(u, u ^ 1) for u in range(UNK)])


def over_chips(value):
    return [value] + [
        lax.ppermute(value, "unk", [(u, u ^ (2 * k)) for u in range(UNK)]) for k in range(1, CHIPS)
    ]


def from_distance(value, k):
    return lax.ppermute(value, "obs", [(o, o ^ k) for o in range(OBS)])


def high_dot(left, right):
    return lax.dot_general(
        left, right, (((0,), (0,)), ((), ())),
        precision=lax.Precision.HIGH, preferred_element_type=jnp.float32,
    )


def local(design, weights):
    obs, unk = lax.axis_index("obs"), lax.axis_index("unk")
    chip, core = unk // 2, unk % 2
    rows = design.shape[0] // 2

    chunk = jnp.where(unk == 0, design[:, :BLOCK], 0.0)
    for j in range(1, CHIPS):
        pairs = [(o * UNK, o * UNK + 2 * j) for o in range(OBS)]
        chunk = chunk + lax.ppermute(design[:, j * BLOCK : (j + 1) * BLOCK], BOTH, pairs)
    lower = swap_cores(chunk[rows:])
    part = jnp.where(core == 0, chunk[:rows], lower)
    mine = jnp.zeros((rows, WIDTH), jnp.float32)
    for k, got in enumerate(over_chips(part)):
        mine = lax.dynamic_update_slice(mine, got, (0, (chip ^ k) * BLOCK))
    other = swap_cores(mine)
    weighted = design * weights[:, None]
    first = lax.dynamic_slice_in_dim(weighted, core * rows, rows, 0)
    second = lax.dynamic_slice_in_dim(weighted, (1 - core) * rows, rows, 0)
    first_weights = lax.dynamic_slice_in_dim(weights, core * rows, rows, 0)[:, None]
    second_weights = lax.dynamic_slice_in_dim(weights, (1 - core) * rows, rows, 0)[:, None]

    def strips(values, scale):
        low = lax.dynamic_slice_in_dim(values, unk * STRIP, STRIP, 1)
        high = lax.dynamic_slice_in_dim(values, (2 * UNK - 1 - unk) * STRIP, STRIP, 1)
        return jnp.concatenate([low, high], axis=1) * scale

    strip = high_dot(strips(mine, first_weights), mine) + high_dot(strips(other, second_weights), other)
    cut = (unk * STRIP // BLOCK + 1) * BLOCK
    high = jnp.pad(strip[STRIP:], ((0, 0), (WIDTH, BLOCK)))
    high = lax.dynamic_slice_in_dim(high, WIDTH - cut, WIDTH + BLOCK, 1)
    lanes = lax.broadcasted_iota(jnp.int32, high.shape, 1)
    piece = jnp.where(lanes < cut, jnp.pad(strip[:STRIP], ((0, 0), (0, BLOCK))), high)
    mine, other, piece = lax.optimization_barrier((mine, other, piece))
    for k in (4, 1, 2):
        piece = piece + from_distance(piece, k)
    mine_top = jnp.stack(over_chips(piece))
    other_top = swap_cores(mine_top)

    partial_value = high_dot(first, mine) + high_dot(second, other)
    owned = partial_value.shape[0] // OBS
    sends = [lax.dynamic_slice_in_dim(partial_value, (obs ^ k) * owned, owned, 0) for k in range(OBS)]
    mine_top, other_top, sends = lax.optimization_barrier((mine_top, other_top, sends))
    received = [from_distance(sends[k], k) for k in range(1, OBS)]
    where = jnp.stack([chip, core]).astype(jnp.int32)
    low, inverse = cholesky_parts(where, mine_top, other_top)
    owned_rows = add_all([sends[0]] + received)
    return solve_rows(owned_rows, low, inverse)


def solution(mesh):
    return jax.shard_map(
        local,
        mesh=mesh,
        in_specs=(P("obs", "unk"), P("obs")),
        out_specs=P(("unk", "obs"), None),
        check_vma=False,
    )
```

```python
import jax, jax.numpy as jnp
from jax import lax
from jax.experimental import pallas as pl
from jax.experimental.pallas import tpu as pltpu
from jax.sharding import PartitionSpec as P

BLOCK = 128
SUB = 8
STRIP = 32


def split(x):
    hi = x.astype(jnp.bfloat16)
    return hi, (x - hi.astype(jnp.float32)).astype(jnp.bfloat16)


def dot_t(a, b):
    return lax.dot_general(a, b, (((1,), (1,)), ((), ())), preferred_element_type=jnp.float32)


def dot3_t(a, b):
    (ah, al), (bh, bl) = a, b
    return dot_t(ah, bh) + (dot_t(ah, bl) + dot_t(al, bh))


def on_lanes(value, lane):
    return jnp.broadcast_to(value[:, lane : lane + 1], (SUB, BLOCK))


def invert_diag(block_ref, inv_ref, stage, rows_ref):
    lane = lax.broadcasted_iota(jnp.int32, (SUB, BLOCK), 1)
    panels = BLOCK // SUB
    groups = [block_ref[q * SUB : (q + 1) * SUB, :] for q in range(panels)]
    natural, carried = None, None
    for p in range(panels):
        r0 = p * SUB
        base = (p % 2) * 3 * SUB * SUB
        one = lambda row: stage[pl.ds(base + row, SUB, stride=0), :]
        panel = groups[p]
        columns = [on_lanes(panel, r0 + c) for c in range(SUB)]
        if natural is not None:
            for i in range(SUB):
                stage[base + i * SUB : base + (i + 1) * SUB, :] = on_lanes(natural, r0 + i)
            panel = jnp.where((lane >= r0 - SUB) & (lane < r0), 0.0, panel)
            for k in range(SUB):
                down = stage[pl.ds(base + k, SUB, stride=SUB), :]
                panel = panel - down * carried[k]
                for c in range(SUB):
                    columns[c] = columns[c] - down * one(c * SUB + k)
        inside = (lane >= r0) & (lane < r0 + SUB)
        sub = lax.broadcasted_iota(jnp.int32, (SUB, BLOCK), 0)
        panel = jnp.where(inside, jnp.where(lane == r0 + sub, 1.0, 0.0), panel)
        at = SUB * SUB
        for c in range(SUB):
            stage[base + at + c * SUB : base + at + (c + 1) * SUB, :] = columns[c]
        stage[base + 2 * at : base + 2 * at + SUB, :] = panel
        e = {(i, c): one(at + c * SUB + i) for c in range(SUB) for i in range(c + 1)}
        w = [one(2 * at + i) for i in range(SUB)]
        for c in range(SUB):
            inv = lax.rsqrt(e[c, c])
            w[c] = w[c] * inv
            u = {i: e[c, i] * inv for i in range(c + 1, SUB)}
            for i in range(c + 1, SUB):
                w[i] = w[i] - u[i] * w[c]
                for j in range(i, SUB):
                    e[i, j] = e[i, j] - u[i] * u[j]
            rows_ref[r0 + c : r0 + c + 1, :] = w[c][0:1, :]
        natural, carried = rows_ref[r0 : r0 + SUB, :], w
        inv_ref[r0 : r0 + SUB, :] = jnp.where(lane < r0 + SUB, natural, 0.0)
        if p + 2 < panels:
            for q in range(p + 2, panels):
                spare = 6 * SUB * SUB + (q % 2) * SUB * SUB
                for i in range(SUB):
                    stage[spare + i * SUB : spare + (i + 1) * SUB, :] = on_lanes(natural, q * SUB + i)
                groups[q] = jnp.where(inside, 0.0, groups[q])
                for k in range(SUB):
                    groups[q] = groups[q] - stage[pl.ds(spare + k, SUB, stride=SUB), :] * w[k]


def unpack(where_ref, mine_ref, other_ref, work, pieces):
    count = mine_ref.shape[0]
    chip, core = where_ref[0], where_ref[1]
    for k in range(count):
        pieces[2 * (chip ^ k) + core] = mine_ref[k]
        pieces[2 * (chip ^ k) + 1 - core] = other_ref[k]
    for t in range(2 * count):
        low, high = t * STRIP, (4 * count - 1 - t) * STRIP
        cut, rest = (low // BLOCK + 1) * BLOCK, (high // BLOCK + 1) * BLOCK
        work[low : low + STRIP, :cut] = pieces[t, :, :cut]
        work[high : high + STRIP, :rest] = pieces[t, :, cut:]


def chol_kernel(where_ref, mine_ref, other_ref, low_ref, inv_ref, work, pieces, diag, dinv, hi_ref, lo_ref, stage, rows_ref):
    width = work.shape[0]
    blocks = width // BLOCK
    work[...] = jnp.zeros_like(work)
    unpack(where_ref, mine_ref, other_ref, work, pieces)

    def step(k, _):
        at = pl.multiple_of(k * BLOCK, BLOCK)
        diag[...] = work[pl.ds(at, BLOCK), pl.ds(at, BLOCK)]
        invert_diag(diag, dinv, stage, rows_ref)
        inverse = dinv[...]
        inv_ref[pl.ds(at, BLOCK), :] = inverse
        inverse = split(inverse)
        hi_ref[...] = jnp.zeros_like(hi_ref)
        lo_ref[...] = jnp.zeros_like(lo_ref)

        def below(i, _):
            rows = pl.ds(pl.multiple_of(i * BLOCK, BLOCK), BLOCK)
            new = dot3_t(split(work[rows, pl.ds(at, BLOCK)]), inverse)
            low_ref[rows, pl.ds(at, BLOCK)] = new
            hi, lo = split(new)
            hi_ref[rows, :] = hi
            lo_ref[rows, :] = lo
            return 0

        lax.fori_loop(k + 1, blocks, below, 0)

        def trail(i, _):
            rows = pl.ds(pl.multiple_of(i * BLOCK, BLOCK), BLOCK)
            work[rows, :] = work[rows, :] - dot3_t(
                (hi_ref[rows, :], lo_ref[rows, :]), (hi_ref[...], lo_ref[...])
            )
            return 0

        lax.fori_loop(k + 1, blocks, trail, 0)
        return 0

    lax.fori_loop(0, blocks, step, 0)


def cholesky_parts(where, mine, other):
    count, strip, packed = mine.shape
    width = count * BLOCK
    vmem = pl.BlockSpec(memory_space=pltpu.VMEM)
    return pl.pallas_call(
        chol_kernel,
        out_shape=(
            jax.ShapeDtypeStruct((width, width), jnp.float32),
            jax.ShapeDtypeStruct((width, BLOCK), jnp.float32),
        ),
        in_specs=[pl.BlockSpec(memory_space=pltpu.SMEM), vmem, vmem],
        out_specs=(vmem, vmem),
        scratch_shapes=[
            pltpu.VMEM((width, width), jnp.float32),
            pltpu.VMEM((2 * count, strip, packed), jnp.float32),
            pltpu.VMEM((BLOCK, BLOCK), jnp.float32),
            pltpu.VMEM((BLOCK, BLOCK), jnp.float32),
            pltpu.VMEM((width, BLOCK), jnp.bfloat16),
            pltpu.VMEM((width, BLOCK), jnp.bfloat16),
            pltpu.VMEM((8 * SUB * SUB, BLOCK), jnp.float32),
            pltpu.VMEM((BLOCK, BLOCK), jnp.float32),
        ],
        compiler_params=pltpu.CompilerParams(vmem_limit_bytes=32 << 20),
        cost_estimate=pl.CostEstimate(flops=80_000_000_000, bytes_accessed=8 << 20, transcendentals=0),
    )(where, mine, other)


def solve_kernel(gram_ref, low_ref, inv_ref, out_ref):
    _, width = gram_ref.shape
    blocks = width // BLOCK
    out_ref[...] = gram_ref[...]
    for k in range(blocks):
        cols = slice(k * BLOCK, (k + 1) * BLOCK)
        new = dot3_t(split(out_ref[:, cols]), split(inv_ref[cols, :]))
        out_ref[:, cols] = new
        if k + 1 < blocks:
            rest = slice((k + 1) * BLOCK, width)
            out_ref[:, rest] = out_ref[:, rest] - dot3_t(split(new), split(low_ref[rest, cols]))


def solve_rows(gram, low, inv):
    return pl.pallas_call(
        solve_kernel,
        out_shape=jax.ShapeDtypeStruct(gram.shape, jnp.float32),
        in_specs=[pl.BlockSpec(memory_space=pltpu.VMEM)] * 3,
        out_specs=pl.BlockSpec(memory_space=pltpu.VMEM),
        compiler_params=pltpu.CompilerParams(vmem_limit_bytes=24 << 20),
    )(gram, low, inv)


BOTH = ("obs", "unk")
OBS, UNK = 8, 16
CHIPS = UNK // 2
WIDTH = 1024


def add_all(parts):
    total = parts[0]
    for part in parts[1:]:
        total = total + part
    return total


def swap_cores(value):
    return lax.ppermute(value, "unk", [(u, u ^ 1) for u in range(UNK)])


def over_chips(value):
    return [value] + [
        lax.ppermute(value, "unk", [(u, u ^ (2 * k)) for u in range(UNK)]) for k in range(1, CHIPS)
    ]


def from_distance(value, k):
    return lax.ppermute(value, "obs", [(o, o ^ k) for o in range(OBS)])


def high_dot(left, right):
    return lax.dot_general(
        left, right, (((0,), (0,)), ((), ())),
        precision=lax.Precision.HIGH, preferred_element_type=jnp.float32,
    )


def local(design, weights):
    obs, unk = lax.axis_index("obs"), lax.axis_index("unk")
    chip, core = unk // 2, unk % 2
    rows = design.shape[0] // 2

    chunk = jnp.where(unk == 0, design[:, :BLOCK], 0.0)
    for j in range(1, CHIPS):
        pairs = [(o * UNK, o * UNK + 2 * j) for o in range(OBS)]
        chunk = chunk + lax.ppermute(design[:, j * BLOCK : (j + 1) * BLOCK], BOTH, pairs)
    lower = swap_cores(chunk[rows:])
    part = jnp.where(core == 0, chunk[:rows], lower)
    mine = jnp.zeros((rows, WIDTH), jnp.float32)
    for k, got in enumerate(over_chips(part)):
        mine = lax.dynamic_update_slice(mine, got, (0, (chip ^ k) * BLOCK))
    other = swap_cores(mine)
    weighted = design * weights[:, None]
    first = lax.dynamic_slice_in_dim(weighted, core * rows, rows, 0)
    second = lax.dynamic_slice_in_dim(weighted, (1 - core) * rows, rows, 0)
    first_weights = lax.dynamic_slice_in_dim(weights, core * rows, rows, 0)[:, None]
    second_weights = lax.dynamic_slice_in_dim(weights, (1 - core) * rows, rows, 0)[:, None]

    def strips(values, scale):
        low = lax.dynamic_slice_in_dim(values, unk * STRIP, STRIP, 1)
        high = lax.dynamic_slice_in_dim(values, (2 * UNK - 1 - unk) * STRIP, STRIP, 1)
        return jnp.concatenate([low, high], axis=1) * scale

    strip = high_dot(strips(mine, first_weights), mine) + high_dot(strips(other, second_weights), other)
    cut = (unk * STRIP // BLOCK + 1) * BLOCK
    high = jnp.pad(strip[STRIP:], ((0, 0), (WIDTH, BLOCK)))
    high = lax.dynamic_slice_in_dim(high, WIDTH - cut, WIDTH + BLOCK, 1)
    lanes = lax.broadcasted_iota(jnp.int32, high.shape, 1)
    piece = jnp.where(lanes < cut, jnp.pad(strip[:STRIP], ((0, 0), (0, BLOCK))), high)
    partial_value = high_dot(first, mine)
    piece, partial_value, other = lax.optimization_barrier((piece, partial_value, other))
    came = from_distance(piece, 4)
    partial_value = partial_value + high_dot(second, other)
    piece, partial_value = lax.optimization_barrier((piece + came, partial_value))
    came = from_distance(piece, 1)
    owned = partial_value.shape[0] // OBS
    sends = [lax.dynamic_slice_in_dim(partial_value, (obs ^ k) * owned, owned, 0) for k in range(OBS)]
    piece, sends = lax.optimization_barrier((piece + came, sends))
    came = from_distance(piece, 2)
    piece = piece + came
    received = []
    for k in range(1, OBS):
        received.append(from_distance(sends[k], k))
    gathered = over_chips(piece)
    mine_top = jnp.stack(gathered)
    other_top = swap_cores(mine_top)
    where = jnp.stack([chip, core]).astype(jnp.int32)
    low, inverse = cholesky_parts(where, mine_top, other_top)
    owned_rows = add_all([sends[0]] + received)
    return solve_rows(owned_rows, low, inverse)


def solution(mesh):
    return jax.shard_map(
        local,
        mesh=mesh,
        in_specs=(P("obs", "unk"), P("obs")),
        out_specs=P(("unk", "obs"), None),
        check_vma=False,
    )
```

```python
import jax, jax.numpy as jnp
from jax import lax
from jax.experimental import pallas as pl
from jax.experimental.pallas import tpu as pltpu
from jax.sharding import PartitionSpec as P

BLOCK = 128
SUB = 8
STRIP = 64


def split(x):
    hi = x.astype(jnp.bfloat16)
    return hi, (x - hi.astype(jnp.float32)).astype(jnp.bfloat16)


def dot_t(a, b):
    return lax.dot_general(a, b, (((1,), (1,)), ((), ())), preferred_element_type=jnp.float32)


def dot3_t(a, b):
    (ah, al), (bh, bl) = a, b
    return dot_t(ah, bh) + (dot_t(ah, bl) + dot_t(al, bh))


def on_lanes(value, lane):
    return jnp.broadcast_to(value[:, lane : lane + 1], (SUB, BLOCK))


def invert_diag(block_ref, inv_ref, stage, rows_ref):
    lane = lax.broadcasted_iota(jnp.int32, (SUB, BLOCK), 1)
    panels = BLOCK // SUB
    groups = [block_ref[q * SUB : (q + 1) * SUB, :] for q in range(panels)]
    natural, carried = None, None
    for p in range(panels):
        r0 = p * SUB
        base = (p % 2) * 3 * SUB * SUB
        one = lambda row: stage[pl.ds(base + row, SUB, stride=0), :]
        panel = groups[p]
        columns = [on_lanes(panel, r0 + c) for c in range(SUB)]
        if natural is not None:
            for i in range(SUB):
                stage[base + i * SUB : base + (i + 1) * SUB, :] = on_lanes(natural, r0 + i)
            panel = jnp.where((lane >= r0 - SUB) & (lane < r0), 0.0, panel)
            for k in range(SUB):
                down = stage[pl.ds(base + k, SUB, stride=SUB), :]
                panel = panel - down * carried[k]
                for c in range(SUB):
                    columns[c] = columns[c] - down * one(c * SUB + k)
        inside = (lane >= r0) & (lane < r0 + SUB)
        sub = lax.broadcasted_iota(jnp.int32, (SUB, BLOCK), 0)
        panel = jnp.where(inside, jnp.where(lane == r0 + sub, 1.0, 0.0), panel)
        at = SUB * SUB
        for c in range(SUB):
            stage[base + at + c * SUB : base + at + (c + 1) * SUB, :] = columns[c]
        stage[base + 2 * at : base + 2 * at + SUB, :] = panel
        e = {(i, c): one(at + c * SUB + i) for c in range(SUB) for i in range(c + 1)}
        w = [one(2 * at + i) for i in range(SUB)]
        for c in range(SUB):
            inv = lax.rsqrt(e[c, c])
            w[c] = w[c] * inv
            u = {i: e[c, i] * inv for i in range(c + 1, SUB)}
            for i in range(c + 1, SUB):
                w[i] = w[i] - u[i] * w[c]
                for j in range(i, SUB):
                    e[i, j] = e[i, j] - u[i] * u[j]
            rows_ref[r0 + c : r0 + c + 1, :] = w[c][0:1, :]
        natural, carried = rows_ref[r0 : r0 + SUB, :], w
        inv_ref[r0 : r0 + SUB, :] = jnp.where(lane < r0 + SUB, natural, 0.0)
        if p + 2 < panels:
            for q in range(p + 2, panels):
                spare = 6 * SUB * SUB + (q % 2) * SUB * SUB
                for i in range(SUB):
                    stage[spare + i * SUB : spare + (i + 1) * SUB, :] = on_lanes(natural, q * SUB + i)
                groups[q] = jnp.where(inside, 0.0, groups[q])
                for k in range(SUB):
                    groups[q] = groups[q] - stage[pl.ds(spare + k, SUB, stride=SUB), :] * w[k]


def unpack(where_ref, mine_ref, other_ref, work, pieces):
    count = mine_ref.shape[0]
    chip, core = where_ref[0], where_ref[1]
    for k in range(count):
        pieces[2 * (chip ^ k) + core] = mine_ref[k]
        pieces[2 * (chip ^ k) + 1 - core] = other_ref[k]
    for t in range(2 * count):
        low, high = t * STRIP, (4 * count - 1 - t) * STRIP
        cut, rest = (low // BLOCK + 1) * BLOCK, (high // BLOCK + 1) * BLOCK
        work[low : low + STRIP, :cut] = pieces[t, :, :cut]
        work[high : high + STRIP, :rest] = pieces[t, :, cut:]


def chol_kernel(where_ref, mine_ref, other_ref, low_ref, inv_ref, work, pieces, diag, dinv, hi_ref, lo_ref, stage, rows_ref):
    width = work.shape[0]
    blocks = width // BLOCK
    work[...] = jnp.zeros_like(work)
    unpack(where_ref, mine_ref, other_ref, work, pieces)

    def step(k, _):
        at = pl.multiple_of(k * BLOCK, BLOCK)
        diag[...] = work[pl.ds(at, BLOCK), pl.ds(at, BLOCK)]
        invert_diag(diag, dinv, stage, rows_ref)
        inverse = dinv[...]
        inv_ref[pl.ds(at, BLOCK), :] = inverse
        inverse = split(inverse)
        hi_ref[...] = jnp.zeros_like(hi_ref)
        lo_ref[...] = jnp.zeros_like(lo_ref)

        def below(i, _):
            rows = pl.ds(pl.multiple_of(i * BLOCK, BLOCK), BLOCK)
            new = dot3_t(split(work[rows, pl.ds(at, BLOCK)]), inverse)
            low_ref[rows, pl.ds(at, BLOCK)] = new
            hi, lo = split(new)
            hi_ref[rows, :] = hi
            lo_ref[rows, :] = lo
            return 0

        lax.fori_loop(k + 1, blocks, below, 0)

        def trail(i, _):
            rows = pl.ds(pl.multiple_of(i * BLOCK, BLOCK), BLOCK)
            work[rows, :] = work[rows, :] - dot3_t(
                (hi_ref[rows, :], lo_ref[rows, :]), (hi_ref[...], lo_ref[...])
            )
            return 0

        lax.fori_loop(k + 1, blocks, trail, 0)
        return 0

    lax.fori_loop(0, blocks, step, 0)


def cholesky_parts(where, mine, other):
    count, strip, packed = mine.shape
    width = 4 * count * strip
    vmem = pl.BlockSpec(memory_space=pltpu.VMEM)
    return pl.pallas_call(
        chol_kernel,
        out_shape=(
            jax.ShapeDtypeStruct((width, width), jnp.float32),
            jax.ShapeDtypeStruct((width, BLOCK), jnp.float32),
        ),
        in_specs=[pl.BlockSpec(memory_space=pltpu.SMEM), vmem, vmem],
        out_specs=(vmem, vmem),
        scratch_shapes=[
            pltpu.VMEM((width, width), jnp.float32),
            pltpu.VMEM((2 * count, strip, packed), jnp.float32),
            pltpu.VMEM((BLOCK, BLOCK), jnp.float32),
            pltpu.VMEM((BLOCK, BLOCK), jnp.float32),
            pltpu.VMEM((width, BLOCK), jnp.bfloat16),
            pltpu.VMEM((width, BLOCK), jnp.bfloat16),
            pltpu.VMEM((8 * SUB * SUB, BLOCK), jnp.float32),
            pltpu.VMEM((BLOCK, BLOCK), jnp.float32),
        ],
        compiler_params=pltpu.CompilerParams(vmem_limit_bytes=32 << 20),
        cost_estimate=pl.CostEstimate(flops=80_000_000_000, bytes_accessed=8 << 20, transcendentals=0),
    )(where, mine, other)


def solve_kernel(gram_ref, low_ref, inv_ref, out_ref):
    _, width = gram_ref.shape
    blocks = width // BLOCK
    out_ref[...] = gram_ref[...]
    for k in range(blocks):
        cols = slice(k * BLOCK, (k + 1) * BLOCK)
        new = dot3_t(split(out_ref[:, cols]), split(inv_ref[cols, :]))
        out_ref[:, cols] = new
        if k + 1 < blocks:
            rest = slice((k + 1) * BLOCK, width)
            out_ref[:, rest] = out_ref[:, rest] - dot3_t(split(new), split(low_ref[rest, cols]))


def solve_rows(gram, low, inv):
    return pl.pallas_call(
        solve_kernel,
        out_shape=jax.ShapeDtypeStruct(gram.shape, jnp.float32),
        in_specs=[pl.BlockSpec(memory_space=pltpu.VMEM)] * 3,
        out_specs=pl.BlockSpec(memory_space=pltpu.VMEM),
        compiler_params=pltpu.CompilerParams(vmem_limit_bytes=24 << 20),
    )(gram, low, inv)


BOTH = ("obs", "unk")
OBS, UNK = 8, 16
CHIPS = UNK // 2
LINE = 4
STRIPS = 2 * LINE
WIDTH = 1024


def add_all(parts):
    total = parts[0]
    for part in parts[1:]:
        total = total + part
    return total


def swap_cores(value):
    return lax.ppermute(value, "unk", [(u, u ^ 1) for u in range(UNK)])


def over_chips(value, chips):
    return [value] + [
        lax.ppermute(value, "unk", [(u, u ^ (2 * k)) for u in range(UNK)]) for k in range(1, chips)
    ]


def from_distance(value, k):
    return lax.ppermute(value, "obs", [(o, o ^ k) for o in range(OBS)])


def high_dot(left, right):
    return lax.dot_general(
        left, right, (((0,), (0,)), ((), ())),
        precision=lax.Precision.HIGH, preferred_element_type=jnp.float32,
    )


def local(design, weights):
    obs, unk = lax.axis_index("obs"), lax.axis_index("unk")
    chip, core = unk // 2, unk % 2
    rows = design.shape[0] // 2

    chunk = jnp.where(unk == 0, design[:, :BLOCK], 0.0)
    for j in range(1, CHIPS):
        pairs = [(o * UNK, o * UNK + 2 * j) for o in range(OBS)]
        chunk = chunk + lax.ppermute(design[:, j * BLOCK : (j + 1) * BLOCK], BOTH, pairs)
    weighted = design * weights[:, None]
    chunk, weighted = lax.optimization_barrier((chunk, weighted))
    lower = swap_cores(chunk[rows:])
    part = jnp.where(core == 0, chunk[:rows], lower)
    mine = jnp.zeros((rows, WIDTH), jnp.float32)
    for k, got in enumerate(over_chips(part, CHIPS)):
        mine = lax.dynamic_update_slice(mine, got, (0, (chip ^ k) * BLOCK))
    other = swap_cores(mine)
    first = lax.dynamic_slice_in_dim(weighted, core * rows, rows, 0)
    second = lax.dynamic_slice_in_dim(weighted, (1 - core) * rows, rows, 0)
    first_weights = lax.dynamic_slice_in_dim(weights, core * rows, rows, 0)[:, None]
    second_weights = lax.dynamic_slice_in_dim(weights, (1 - core) * rows, rows, 0)[:, None]

    spot = chip % LINE * 2 + core

    def strips(values, scale):
        low = lax.dynamic_slice_in_dim(values, spot * STRIP, STRIP, 1)
        high = lax.dynamic_slice_in_dim(values, (2 * STRIPS - 1 - spot) * STRIP, STRIP, 1)
        return jnp.concatenate([low, high], axis=1) * scale

    strip = high_dot(strips(mine, first_weights), mine)
    strip, other = lax.optimization_barrier((strip, other))
    strip = strip + high_dot(strips(other, second_weights), other)
    cut = (spot * STRIP // BLOCK + 1) * BLOCK
    high = jnp.pad(strip[STRIP:], ((0, 0), (WIDTH, BLOCK)))
    high = lax.dynamic_slice_in_dim(high, WIDTH - cut, WIDTH + BLOCK, 1)
    lanes = lax.broadcasted_iota(jnp.int32, high.shape, 1)
    piece = jnp.where(lanes < cut, jnp.pad(strip[:STRIP], ((0, 0), (0, BLOCK))), high)
    piece, mine, other = lax.optimization_barrier((piece, mine, other))
    came = from_distance(piece, 4)
    partial_value = high_dot(first, mine)
    piece, partial_value, other = lax.optimization_barrier((piece + came, partial_value, other))
    came = from_distance(piece, 1)
    partial_value = partial_value + high_dot(second, other)
    owned = partial_value.shape[0] // OBS
    sends = [lax.dynamic_slice_in_dim(partial_value, (obs ^ k) * owned, owned, 0) for k in range(OBS)]
    piece, sends = lax.optimization_barrier((piece + came, sends))
    came = from_distance(piece, 2)
    piece = piece + came
    received = []
    for k in range(1, OBS):
        received.append(from_distance(sends[k], k))
    gathered = over_chips(piece, LINE)
    mine_top = jnp.stack(gathered)
    other_top = swap_cores(mine_top)
    where = jnp.stack([chip % LINE, core]).astype(jnp.int32)
    low, inverse = cholesky_parts(where, mine_top, other_top)
    owned_rows = add_all([sends[0]] + received)
    return solve_rows(owned_rows, low, inverse)


def solution(mesh):
    return jax.shard_map(
        local,
        mesh=mesh,
        in_specs=(P("obs", "unk"), P("obs")),
        out_specs=P(("unk", "obs"), None),
        check_vma=False,
    )
```

```python
import jax, jax.numpy as jnp
from jax import lax
from jax.experimental import pallas as pl
from jax.experimental.pallas import tpu as pltpu
from jax.sharding import PartitionSpec as P

BLOCK = 128
SUB = 8
STRIP = 64


def split(x):
    hi = x.astype(jnp.bfloat16)
    return hi, (x - hi.astype(jnp.float32)).astype(jnp.bfloat16)


def dot_t(a, b):
    return lax.dot_general(a, b, (((1,), (1,)), ((), ())), preferred_element_type=jnp.float32)


def dot3_t(a, b):
    (ah, al), (bh, bl) = a, b
    return dot_t(ah, bh) + (dot_t(ah, bl) + dot_t(al, bh))


def on_lanes(value, lane):
    return jnp.broadcast_to(value[:, lane : lane + 1], (SUB, BLOCK))


def invert_diag(block_ref, inv_ref, stage, rows_ref):
    lane = lax.broadcasted_iota(jnp.int32, (SUB, BLOCK), 1)
    panels = BLOCK // SUB
    groups = [block_ref[q * SUB : (q + 1) * SUB, :] for q in range(panels)]
    natural, carried = None, None
    for p in range(panels):
        r0 = p * SUB
        base = (p % 2) * 3 * SUB * SUB
        one = lambda row: stage[pl.ds(base + row, SUB, stride=0), :]
        panel = groups[p]
        columns = [on_lanes(panel, r0 + c) for c in range(SUB)]
        if natural is not None:
            for i in range(SUB):
                stage[base + i * SUB : base + (i + 1) * SUB, :] = on_lanes(natural, r0 + i)
            panel = jnp.where((lane >= r0 - SUB) & (lane < r0), 0.0, panel)
            for k in range(SUB):
                down = stage[pl.ds(base + k, SUB, stride=SUB), :]
                panel = panel - down * carried[k]
                for c in range(SUB):
                    columns[c] = columns[c] - down * one(c * SUB + k)
        inside = (lane >= r0) & (lane < r0 + SUB)
        sub = lax.broadcasted_iota(jnp.int32, (SUB, BLOCK), 0)
        panel = jnp.where(inside, jnp.where(lane == r0 + sub, 1.0, 0.0), panel)
        at = SUB * SUB
        for c in range(SUB):
            stage[base + at + c * SUB : base + at + (c + 1) * SUB, :] = columns[c]
        stage[base + 2 * at : base + 2 * at + SUB, :] = panel
        e = {(i, c): one(at + c * SUB + i) for c in range(SUB) for i in range(c + 1)}
        w = [one(2 * at + i) for i in range(SUB)]
        for c in range(SUB):
            inv = lax.rsqrt(e[c, c])
            w[c] = w[c] * inv
            u = {i: e[c, i] * inv for i in range(c + 1, SUB)}
            for i in range(c + 1, SUB):
                w[i] = w[i] - u[i] * w[c]
                for j in range(i, SUB):
                    e[i, j] = e[i, j] - u[i] * u[j]
            rows_ref[r0 + c : r0 + c + 1, :] = w[c][0:1, :]
        natural, carried = rows_ref[r0 : r0 + SUB, :], w
        inv_ref[r0 : r0 + SUB, :] = jnp.where(lane < r0 + SUB, natural, 0.0)
        if p + 2 < panels:
            for q in range(p + 2, panels):
                spare = 6 * SUB * SUB + (q % 2) * SUB * SUB
                for i in range(SUB):
                    stage[spare + i * SUB : spare + (i + 1) * SUB, :] = on_lanes(natural, q * SUB + i)
                groups[q] = jnp.where(inside, 0.0, groups[q])
                for k in range(SUB):
                    groups[q] = groups[q] - stage[pl.ds(spare + k, SUB, stride=SUB), :] * w[k]


def unpack(where_ref, mine_ref, other_ref, work, pieces):
    count = mine_ref.shape[0]
    chip, core = where_ref[0], where_ref[1]
    for k in range(count):
        pieces[2 * (chip ^ k) + core] = mine_ref[k]
        pieces[2 * (chip ^ k) + 1 - core] = other_ref[k]
    for t in range(2 * count):
        low, high = t * STRIP, (4 * count - 1 - t) * STRIP
        cut, rest = (low // BLOCK + 1) * BLOCK, (high // BLOCK + 1) * BLOCK
        work[low : low + STRIP, :cut] = pieces[t, :, :cut]
        work[high : high + STRIP, :rest] = pieces[t, :, cut:]


def chol_kernel(where_ref, mine_ref, other_ref, low_ref, inv_ref, work, pieces, diag, dinv, hi_ref, lo_ref, stage, rows_ref):
    width = work.shape[0]
    blocks = width // BLOCK
    work[...] = jnp.zeros_like(work)
    unpack(where_ref, mine_ref, other_ref, work, pieces)

    def step(k, _):
        at = pl.multiple_of(k * BLOCK, BLOCK)
        diag[...] = work[pl.ds(at, BLOCK), pl.ds(at, BLOCK)]
        invert_diag(diag, dinv, stage, rows_ref)
        inverse = dinv[...]
        inv_ref[pl.ds(at, BLOCK), :] = inverse
        inverse = split(inverse)
        hi_ref[...] = jnp.zeros_like(hi_ref)
        lo_ref[...] = jnp.zeros_like(lo_ref)

        def below(i, _):
            rows = pl.ds(pl.multiple_of(i * BLOCK, BLOCK), BLOCK)
            new = dot3_t(split(work[rows, pl.ds(at, BLOCK)]), inverse)
            low_ref[rows, pl.ds(at, BLOCK)] = new
            hi, lo = split(new)
            hi_ref[rows, :] = hi
            lo_ref[rows, :] = lo
            return 0

        lax.fori_loop(k + 1, blocks, below, 0)

        def trail(i, _):
            rows = pl.ds(pl.multiple_of(i * BLOCK, BLOCK), BLOCK)
            work[rows, :] = work[rows, :] - dot3_t(
                (hi_ref[rows, :], lo_ref[rows, :]), (hi_ref[...], lo_ref[...])
            )
            return 0

        lax.fori_loop(k + 1, blocks, trail, 0)
        return 0

    lax.fori_loop(0, blocks, step, 0)


def cholesky_parts(where, mine, other):
    count, strip, packed = mine.shape
    width = 4 * count * strip
    vmem = pl.BlockSpec(memory_space=pltpu.VMEM)
    return pl.pallas_call(
        chol_kernel,
        out_shape=(
            jax.ShapeDtypeStruct((width, width), jnp.float32),
            jax.ShapeDtypeStruct((width, BLOCK), jnp.float32),
        ),
        in_specs=[pl.BlockSpec(memory_space=pltpu.SMEM), vmem, vmem],
        out_specs=(vmem, vmem),
        scratch_shapes=[
            pltpu.VMEM((width, width), jnp.float32),
            pltpu.VMEM((2 * count, strip, packed), jnp.float32),
            pltpu.VMEM((BLOCK, BLOCK), jnp.float32),
            pltpu.VMEM((BLOCK, BLOCK), jnp.float32),
            pltpu.VMEM((width, BLOCK), jnp.bfloat16),
            pltpu.VMEM((width, BLOCK), jnp.bfloat16),
            pltpu.VMEM((8 * SUB * SUB, BLOCK), jnp.float32),
            pltpu.VMEM((BLOCK, BLOCK), jnp.float32),
        ],
        compiler_params=pltpu.CompilerParams(vmem_limit_bytes=32 << 20),
        cost_estimate=pl.CostEstimate(flops=80_000_000_000, bytes_accessed=8 << 20, transcendentals=0),
    )(where, mine, other)


def solve_kernel(gram_ref, low_ref, inv_ref, out_ref):
    _, width = gram_ref.shape
    blocks = width // BLOCK
    out_ref[...] = gram_ref[...]
    for k in range(blocks):
        cols = slice(k * BLOCK, (k + 1) * BLOCK)
        new = dot3_t(split(out_ref[:, cols]), split(inv_ref[cols, :]))
        out_ref[:, cols] = new
        if k + 1 < blocks:
            rest = slice((k + 1) * BLOCK, width)
            out_ref[:, rest] = out_ref[:, rest] - dot3_t(split(new), split(low_ref[rest, cols]))


def solve_rows(gram, low, inv):
    return pl.pallas_call(
        solve_kernel,
        out_shape=jax.ShapeDtypeStruct(gram.shape, jnp.float32),
        in_specs=[pl.BlockSpec(memory_space=pltpu.VMEM)] * 3,
        out_specs=pl.BlockSpec(memory_space=pltpu.VMEM),
        compiler_params=pltpu.CompilerParams(vmem_limit_bytes=24 << 20),
    )(gram, low, inv)


BOTH = ("obs", "unk")
OBS, UNK = 8, 16
CHIPS = UNK // 2
LINE = 4
STRIPS = 2 * LINE
WIDTH = 1024


def add_all(parts):
    total = parts[0]
    for part in parts[1:]:
        total = total + part
    return total


def swap_cores(value):
    return lax.ppermute(value, "unk", [(u, u ^ 1) for u in range(UNK)])


def over_chips(value, chips):
    return [value] + [
        lax.ppermute(value, "unk", [(u, u ^ (2 * k)) for u in range(UNK)]) for k in range(1, chips)
    ]


def from_distance(value, k):
    return lax.ppermute(value, "obs", [(o, o ^ k) for o in range(OBS)])


def high_dot(left, right):
    return lax.dot_general(
        left, right, (((0,), (0,)), ((), ())),
        precision=lax.Precision.HIGH, preferred_element_type=jnp.float32,
    )


def local(design, weights):
    obs, unk = lax.axis_index("obs"), lax.axis_index("unk")
    chip, core = unk // 2, unk % 2
    rows = design.shape[0] // 2

    chunk = jnp.where(unk == 0, design[:, :BLOCK], 0.0)
    for j in range(1, CHIPS):
        pairs = [(o * UNK, o * UNK + 2 * j) for o in range(OBS)]
        chunk = chunk + lax.ppermute(design[:, j * BLOCK : (j + 1) * BLOCK], BOTH, pairs)

    def core_half(half):
        cut = lambda values: lax.dynamic_slice_in_dim(values, half * rows, rows, 0)
        return cut(design) * cut(weights)[:, None]

    chunk, first, second = lax.optimization_barrier((chunk, core_half(core), core_half(1 - core)))
    lower = swap_cores(chunk[rows:])
    part = jnp.where(core == 0, chunk[:rows], lower)
    mine = jnp.zeros((rows, WIDTH), jnp.float32)
    for k, got in enumerate(over_chips(part, CHIPS)):
        mine = lax.dynamic_update_slice(mine, got, (0, (chip ^ k) * BLOCK))
    other = swap_cores(mine)
    first_weights = lax.dynamic_slice_in_dim(weights, core * rows, rows, 0)[:, None]
    second_weights = lax.dynamic_slice_in_dim(weights, (1 - core) * rows, rows, 0)[:, None]

    spot = chip % LINE * 2 + core

    def strips(values, scale):
        low = lax.dynamic_slice_in_dim(values, spot * STRIP, STRIP, 1)
        high = lax.dynamic_slice_in_dim(values, (2 * STRIPS - 1 - spot) * STRIP, STRIP, 1)
        return jnp.concatenate([low, high], axis=1) * scale

    strip = high_dot(strips(mine, first_weights), mine)
    strip, other = lax.optimization_barrier((strip, other))
    strip = strip + high_dot(strips(other, second_weights), other)
    cut = (spot * STRIP // BLOCK + 1) * BLOCK
    high = jnp.pad(strip[STRIP:], ((0, 0), (WIDTH, BLOCK)))
    high = lax.dynamic_slice_in_dim(high, WIDTH - cut, WIDTH + BLOCK, 1)
    lanes = lax.broadcasted_iota(jnp.int32, high.shape, 1)
    piece = jnp.where(lanes < cut, jnp.pad(strip[:STRIP], ((0, 0), (0, BLOCK))), high)
    piece, mine, other = lax.optimization_barrier((piece, mine, other))
    came = from_distance(piece, 4)
    partial_value = high_dot(first, mine)
    piece, partial_value, other = lax.optimization_barrier((piece + came, partial_value, other))
    came = from_distance(piece, 1)
    partial_value = partial_value + high_dot(second, other)
    owned = partial_value.shape[0] // OBS
    sends = [lax.dynamic_slice_in_dim(partial_value, (obs ^ k) * owned, owned, 0) for k in range(OBS)]
    piece, sends = lax.optimization_barrier((piece + came, sends))
    came = from_distance(piece, 2)
    piece = piece + came
    received = []
    for k in range(1, OBS):
        received.append(from_distance(sends[k], k))
    gathered = over_chips(piece, LINE)
    mine_top = jnp.stack(gathered)
    other_top = swap_cores(mine_top)
    where = jnp.stack([chip % LINE, core]).astype(jnp.int32)
    low, inverse = cholesky_parts(where, mine_top, other_top)
    owned_rows = add_all([sends[0]] + received)
    return solve_rows(owned_rows, low, inverse)


def solution(mesh):
    return jax.shard_map(
        local,
        mesh=mesh,
        in_specs=(P("obs", "unk"), P("obs")),
        out_specs=P(("unk", "obs"), None),
        check_vma=False,
    )
```

```python
import jax, jax.numpy as jnp
from jax import lax
from jax.experimental import pallas as pl
from jax.experimental.pallas import tpu as pltpu
from jax.sharding import PartitionSpec as P

BLOCK = 128
SUB = 8
STRIP = 64


def split(x):
    hi = x.astype(jnp.bfloat16)
    return hi, (x - hi.astype(jnp.float32)).astype(jnp.bfloat16)


def dot_t(a, b):
    return lax.dot_general(a, b, (((1,), (1,)), ((), ())), preferred_element_type=jnp.float32)


def dot3_t(a, b):
    (ah, al), (bh, bl) = a, b
    return dot_t(ah, bh) + (dot_t(ah, bl) + dot_t(al, bh))


def on_lanes(value, lane):
    return jnp.broadcast_to(value[:, lane : lane + 1], (SUB, BLOCK))


def invert_diag(block_ref, inv_ref, stage, rows_ref):
    lane = lax.broadcasted_iota(jnp.int32, (SUB, BLOCK), 1)
    panels = BLOCK // SUB
    groups = [block_ref[q * SUB : (q + 1) * SUB, :] for q in range(panels)]
    natural, carried = None, None
    for p in range(panels):
        r0 = p * SUB
        base = (p % 2) * 3 * SUB * SUB
        one = lambda row: stage[pl.ds(base + row, SUB, stride=0), :]
        panel = groups[p]
        columns = [on_lanes(panel, r0 + c) for c in range(SUB)]
        if natural is not None:
            for i in range(SUB):
                stage[base + i * SUB : base + (i + 1) * SUB, :] = on_lanes(natural, r0 + i)
            panel = jnp.where((lane >= r0 - SUB) & (lane < r0), 0.0, panel)
            for k in range(SUB):
                down = stage[pl.ds(base + k, SUB, stride=SUB), :]
                panel = panel - down * carried[k]
                for c in range(SUB):
                    columns[c] = columns[c] - down * one(c * SUB + k)
        inside = (lane >= r0) & (lane < r0 + SUB)
        sub = lax.broadcasted_iota(jnp.int32, (SUB, BLOCK), 0)
        panel = jnp.where(inside, jnp.where(lane == r0 + sub, 1.0, 0.0), panel)
        at = SUB * SUB
        for c in range(SUB):
            stage[base + at + c * SUB : base + at + (c + 1) * SUB, :] = columns[c]
        stage[base + 2 * at : base + 2 * at + SUB, :] = panel
        e = {(i, c): one(at + c * SUB + i) for c in range(SUB) for i in range(c + 1)}
        w = [one(2 * at + i) for i in range(SUB)]
        for c in range(SUB):
            inv = lax.rsqrt(e[c, c])
            w[c] = w[c] * inv
            u = {i: e[c, i] * inv for i in range(c + 1, SUB)}
            for i in range(c + 1, SUB):
                w[i] = w[i] - u[i] * w[c]
                for j in range(i, SUB):
                    e[i, j] = e[i, j] - u[i] * u[j]
            rows_ref[r0 + c : r0 + c + 1, :] = w[c][0:1, :]
        natural, carried = rows_ref[r0 : r0 + SUB, :], w
        inv_ref[r0 : r0 + SUB, :] = jnp.where(lane < r0 + SUB, natural, 0.0)
        if p + 2 < panels:
            for q in range(p + 2, panels):
                spare = 6 * SUB * SUB + (q % 2) * SUB * SUB
                for i in range(SUB):
                    stage[spare + i * SUB : spare + (i + 1) * SUB, :] = on_lanes(natural, q * SUB + i)
                groups[q] = jnp.where(inside, 0.0, groups[q])
                for k in range(SUB):
                    groups[q] = groups[q] - stage[pl.ds(spare + k, SUB, stride=SUB), :] * w[k]


def unpack(where_ref, mine_ref, other_ref, work, pieces):
    count = mine_ref.shape[0]
    chip, core = where_ref[0], where_ref[1]
    for k in range(count):
        pieces[2 * (chip ^ k) + core] = mine_ref[k]
        pieces[2 * (chip ^ k) + 1 - core] = other_ref[k]
    for t in range(2 * count):
        low, high = t * STRIP, (4 * count - 1 - t) * STRIP
        cut, rest = (low // BLOCK + 1) * BLOCK, (high // BLOCK + 1) * BLOCK
        work[low : low + STRIP, :cut] = pieces[t, :, :cut]
        work[high : high + STRIP, :rest] = pieces[t, :, cut:]


def chol_kernel(where_ref, mine_ref, other_ref, low_ref, inv_ref, work, pieces, diag, dinv, left_ref, right_ref, stage, rows_ref):
    work[...] = jnp.zeros_like(work)
    unpack(where_ref, mine_ref, other_ref, work, pieces)
    factor_steps(low_ref, inv_ref, work, diag, dinv, left_ref, right_ref, stage, rows_ref)


def factor_steps(low_ref, inv_ref, work, diag, dinv, left_ref, right_ref, stage, rows_ref):
    width = work.shape[0]
    blocks = width // BLOCK
    left_ref[...] = jnp.zeros_like(left_ref)
    right_ref[...] = jnp.zeros_like(right_ref)

    def step(k, _):
        at = pl.multiple_of(k * BLOCK, BLOCK)
        after = pl.multiple_of(jnp.minimum(k + 1, blocks - 1) * BLOCK, BLOCK)
        diag[...] = work[pl.ds(at, BLOCK), pl.ds(at, BLOCK)]
        for i in range(blocks):
            rows = slice(i * BLOCK, (i + 1) * BLOCK)
            work[rows, :] = work[rows, :] - dot_t(left_ref[rows, :], right_ref[...])
        invert_diag(diag, dinv, stage, rows_ref)
        inverse = dinv[...]
        inv_ref[pl.ds(at, BLOCK), :] = inverse
        hi, lo = split(inverse)
        inverse = jnp.concatenate([hi, lo, hi], axis=1)
        for i in range(blocks):
            rows = slice(i * BLOCK, (i + 1) * BLOCK)
            hi, lo = split(work[rows, pl.ds(at, BLOCK)])
            new = dot_t(jnp.concatenate([hi, hi, lo], axis=1), inverse)
            new = jnp.where(i > k, new, 0.0)
            low_ref[rows, pl.ds(at, BLOCK)] = new
            hi, lo = split(new)
            left_ref[rows, :] = jnp.concatenate([hi, hi, lo], axis=1)
            right_ref[rows, :] = jnp.concatenate([hi, lo, hi], axis=1)
        ahead = right_ref[pl.ds(after, BLOCK), :]
        for i in range(blocks):
            rows = slice(i * BLOCK, (i + 1) * BLOCK)
            work[rows, pl.ds(after, BLOCK)] = work[rows, pl.ds(after, BLOCK)] - dot_t(left_ref[rows, :], ahead)
        right_ref[pl.ds(after, BLOCK), :] = jnp.zeros_like(ahead)
        return 0

    lax.fori_loop(0, blocks, step, 0)


def cholesky_parts(where, mine, other):
    count, strip, packed = mine.shape
    width = 4 * count * strip
    vmem = pl.BlockSpec(memory_space=pltpu.VMEM)
    return pl.pallas_call(
        chol_kernel,
        out_shape=(
            jax.ShapeDtypeStruct((width, width), jnp.float32),
            jax.ShapeDtypeStruct((width, BLOCK), jnp.float32),
        ),
        in_specs=[pl.BlockSpec(memory_space=pltpu.SMEM), vmem, vmem],
        out_specs=(vmem, vmem),
        scratch_shapes=[
            pltpu.VMEM((width, width), jnp.float32),
            pltpu.VMEM((2 * count, strip, packed), jnp.float32),
            pltpu.VMEM((BLOCK, BLOCK), jnp.float32),
            pltpu.VMEM((BLOCK, BLOCK), jnp.float32),
            pltpu.VMEM((width, 3 * BLOCK), jnp.bfloat16),
            pltpu.VMEM((width, 3 * BLOCK), jnp.bfloat16),
            pltpu.VMEM((8 * SUB * SUB, BLOCK), jnp.float32),
            pltpu.VMEM((BLOCK, BLOCK), jnp.float32),
        ],
        compiler_params=pltpu.CompilerParams(vmem_limit_bytes=32 << 20),
        cost_estimate=pl.CostEstimate(flops=80_000_000_000, bytes_accessed=8 << 20, transcendentals=0),
    )(where, mine, other)


def solve_kernel(where_ref, gram_ref, low_ref, inv_ref, out_ref):
    _, width = gram_ref.shape
    blocks, half = width // BLOCK, width // 2
    plane = where_ref[2]
    out_ref[:, pl.ds(pl.multiple_of(plane * half, half), half)] = gram_ref[:, :half]
    out_ref[:, pl.ds(pl.multiple_of((1 - plane) * half, half), half)] = gram_ref[:, half:]
    for k in range(blocks):
        cols = slice(k * BLOCK, (k + 1) * BLOCK)
        new = dot3_t(split(out_ref[:, cols]), split(inv_ref[cols, :]))
        out_ref[:, cols] = new
        if k + 1 < blocks:
            rest = slice((k + 1) * BLOCK, width)
            out_ref[:, rest] = out_ref[:, rest] - dot3_t(split(new), split(low_ref[rest, cols]))


def solve_rows(where, gram, low, inv):
    return pl.pallas_call(
        solve_kernel,
        out_shape=jax.ShapeDtypeStruct(gram.shape, jnp.float32),
        in_specs=[pl.BlockSpec(memory_space=pltpu.SMEM)] + [pl.BlockSpec(memory_space=pltpu.VMEM)] * 3,
        out_specs=pl.BlockSpec(memory_space=pltpu.VMEM),
        compiler_params=pltpu.CompilerParams(vmem_limit_bytes=24 << 20),
    )(where, gram, low, inv)


BOTH = ("obs", "unk")
OBS, UNK = 8, 16
CHIPS = UNK // 2
LINE = 4
STRIPS = 2 * LINE
WIDTH = 1024


def add_all(parts):
    total = parts[0]
    for part in parts[1:]:
        total = total + part
    return total


def swap_cores(value):
    return lax.ppermute(value, "unk", [(u, u ^ 1) for u in range(UNK)])


def over_chips(value, chips):
    got = [value]
    for k in range(1, chips):
        got.append(lax.ppermute(value, "unk", [(u, u ^ (2 * k)) for u in range(UNK)]))
    return got


def from_distance(value, k):
    return lax.ppermute(value, "obs", [(o, o ^ k) for o in range(OBS)])


def high_dot(left, right):
    return lax.dot_general(
        left, right, (((0,), (0,)), ((), ())),
        precision=lax.Precision.HIGH, preferred_element_type=jnp.float32,
    )


def local(design, weights):
    obs, unk = lax.axis_index("obs"), lax.axis_index("unk")
    chip, core = unk // 2, unk % 2
    rows = design.shape[0] // 2

    chunk = jnp.where(unk == 0, design[:, :BLOCK], 0.0)
    for j in range(1, CHIPS):
        pairs = [(o * UNK, o * UNK + 2 * j) for o in range(OBS)]
        chunk = chunk + lax.ppermute(design[:, j * BLOCK : (j + 1) * BLOCK], BOTH, pairs)

    def core_half(half):
        cut = lambda values: lax.dynamic_slice_in_dim(values, half * rows, rows, 0)
        return cut(design) * cut(weights)[:, None]

    chunk, first, second = lax.optimization_barrier((chunk, core_half(core), core_half(1 - core)))
    lower = swap_cores(chunk[rows:])
    part = jnp.where(core == 0, chunk[:rows], lower)
    plane, place = chip // LINE, chip % LINE
    got = over_chips(part, CHIPS)

    def half_of(parts):
        half = jnp.zeros((rows, WIDTH // 2), jnp.float32)
        for k, value in enumerate(parts):
            half = lax.dynamic_update_slice(half, value, (0, (place ^ k) * BLOCK))
        return half

    near, far = half_of(got[:LINE]), half_of(got[LINE:])
    near_other = swap_cores(near)
    near_value = high_dot(first, near) + high_dot(second, near_other)
    far, near_value = lax.optimization_barrier((far, near_value))
    far_other = swap_cores(far)
    first_weights = lax.dynamic_slice_in_dim(weights, core * rows, rows, 0)[:, None]
    second_weights = lax.dynamic_slice_in_dim(weights, (1 - core) * rows, rows, 0)[:, None]

    spot = place * 2 + core

    def strips(near, far, scale):
        left, right = jnp.where(plane == 0, near, far), jnp.where(plane == 0, far, near)
        low = lax.dynamic_slice_in_dim(left, spot * STRIP, STRIP, 1)
        high = lax.dynamic_slice_in_dim(right, (STRIPS - 1 - spot) * STRIP, STRIP, 1)
        return jnp.concatenate([low, high], axis=1) * scale

    chosen = strips(near, far, first_weights)
    strip = (high_dot(chosen, near), high_dot(chosen, far))
    strip, far_other = lax.optimization_barrier((strip, far_other))
    chosen = strips(near_other, far_other, second_weights)
    strip = jnp.concatenate([
        strip[0] + high_dot(chosen, near_other), strip[1] + high_dot(chosen, far_other),
    ], axis=1)
    strip = jnp.where(plane == 0, strip, jnp.roll(strip, WIDTH // 2, axis=1))
    cut = (spot * STRIP // BLOCK + 1) * BLOCK
    high = jnp.pad(strip[STRIP:], ((0, 0), (WIDTH, BLOCK)))
    high = lax.dynamic_slice_in_dim(high, WIDTH - cut, WIDTH + BLOCK, 1)
    lanes = lax.broadcasted_iota(jnp.int32, high.shape, 1)
    piece = jnp.where(lanes < cut, jnp.pad(strip[:STRIP], ((0, 0), (0, BLOCK))), high)
    piece, far, far_other = lax.optimization_barrier((piece, far, far_other))
    came = from_distance(piece, 4)
    far_value = high_dot(first, far)
    piece, far_value, far_other = lax.optimization_barrier((piece + came, far_value, far_other))
    came = from_distance(piece, 1)
    far_value = far_value + high_dot(second, far_other)
    owned = far_value.shape[0] // OBS

    def send_of(k):
        cut = lambda value: lax.dynamic_slice_in_dim(value, (obs ^ k) * owned, owned, 0)
        return jnp.concatenate([cut(near_value), cut(far_value)], axis=1)

    sends = [send_of(k) for k in range(OBS)]
    piece, sends = lax.optimization_barrier((piece + came, sends))
    came = from_distance(piece, 2)
    piece = piece + came
    received = []
    for k in range(1, OBS):
        received.append(from_distance(sends[k], k))
    gathered = over_chips(piece, LINE)
    mine_top = jnp.stack(gathered)
    other_top = swap_cores(mine_top)
    where = jnp.stack([place, core, plane]).astype(jnp.int32)
    low, inverse = cholesky_parts(where, mine_top, other_top)
    owned_rows = add_all([sends[0]] + received)
    return solve_rows(where, owned_rows, low, inverse)


def solution(mesh):
    return jax.shard_map(
        local,
        mesh=mesh,
        in_specs=(P("obs", "unk"), P("obs")),
        out_specs=P(("unk", "obs"), None),
        check_vma=False,
    )
```

```python
import jax, jax.numpy as jnp
from jax import lax
from jax.experimental import pallas as pl
from jax.experimental.pallas import tpu as pltpu
from jax.sharding import PartitionSpec as P

BLOCK = 128
SUB = 8
STRIP = 64


def split(x):
    hi = x.astype(jnp.bfloat16)
    return hi, (x - hi.astype(jnp.float32)).astype(jnp.bfloat16)


def dot_t(a, b):
    return lax.dot_general(a, b, (((1,), (1,)), ((), ())), preferred_element_type=jnp.float32)


def dot3_t(a, b):
    (ah, al), (bh, bl) = a, b
    return dot_t(ah, bh) + (dot_t(ah, bl) + dot_t(al, bh))


def on_lanes(value, lane):
    return jnp.broadcast_to(value[:, lane : lane + 1], (SUB, BLOCK))


def invert_diag(block_ref, inv_ref, stage, rows_ref):
    lane = lax.broadcasted_iota(jnp.int32, (SUB, BLOCK), 1)
    panels = BLOCK // SUB
    groups = [block_ref[q * SUB : (q + 1) * SUB, :] for q in range(panels)]
    natural, carried = None, None
    for p in range(panels):
        r0 = p * SUB
        base = (p % 2) * 3 * SUB * SUB
        one = lambda row: stage[pl.ds(base + row, SUB, stride=0), :]
        panel = groups[p]
        columns = [on_lanes(panel, r0 + c) for c in range(SUB)]
        if natural is not None:
            for i in range(SUB):
                stage[base + i * SUB : base + (i + 1) * SUB, :] = on_lanes(natural, r0 + i)
            panel = jnp.where((lane >= r0 - SUB) & (lane < r0), 0.0, panel)
            for k in range(SUB):
                down = stage[pl.ds(base + k, SUB, stride=SUB), :]
                panel = panel - down * carried[k]
                for c in range(SUB):
                    columns[c] = columns[c] - down * one(c * SUB + k)
        inside = (lane >= r0) & (lane < r0 + SUB)
        sub = lax.broadcasted_iota(jnp.int32, (SUB, BLOCK), 0)
        panel = jnp.where(inside, jnp.where(lane == r0 + sub, 1.0, 0.0), panel)
        at = SUB * SUB
        for c in range(SUB):
            stage[base + at + c * SUB : base + at + (c + 1) * SUB, :] = columns[c]
        stage[base + 2 * at : base + 2 * at + SUB, :] = panel
        e = {(i, c): one(at + c * SUB + i) for c in range(SUB) for i in range(c + 1)}
        w = [one(2 * at + i) for i in range(SUB)]
        for c in range(SUB):
            inv = lax.rsqrt(e[c, c])
            w[c] = w[c] * inv
            u = {i: e[c, i] * inv for i in range(c + 1, SUB)}
            for i in range(c + 1, SUB):
                w[i] = w[i] - u[i] * w[c]
                for j in range(i, SUB):
                    e[i, j] = e[i, j] - u[i] * u[j]
            rows_ref[r0 + c : r0 + c + 1, :] = w[c][0:1, :]
        natural, carried = rows_ref[r0 : r0 + SUB, :], w
        inv_ref[r0 : r0 + SUB, :] = jnp.where(lane < r0 + SUB, natural, 0.0)
        if p + 2 < panels:
            for q in range(p + 2, panels):
                spare = 6 * SUB * SUB + (q % 2) * SUB * SUB
                for i in range(SUB):
                    stage[spare + i * SUB : spare + (i + 1) * SUB, :] = on_lanes(natural, q * SUB + i)
                groups[q] = jnp.where(inside, 0.0, groups[q])
                for k in range(SUB):
                    groups[q] = groups[q] - stage[pl.ds(spare + k, SUB, stride=SUB), :] * w[k]


def unpack(where_ref, mine_ref, other_ref, work, pieces):
    count = mine_ref.shape[0]
    chip, core = where_ref[0], where_ref[1]
    for k in range(count):
        pieces[2 * (chip ^ k) + core] = mine_ref[k]
        pieces[2 * (chip ^ k) + 1 - core] = other_ref[k]
    for t in range(2 * count):
        low, high = t * STRIP, (4 * count - 1 - t) * STRIP
        cut, rest = (low // BLOCK + 1) * BLOCK, (high // BLOCK + 1) * BLOCK
        work[low : low + STRIP, :cut] = pieces[t, :, :cut]
        work[high : high + STRIP, :rest] = pieces[t, :, cut:]


def chol_kernel(where_ref, mine_ref, other_ref, low_ref, inv_ref, work, pieces, diag, dinv, left_ref, right_ref, stage, rows_ref):
    work[...] = jnp.zeros_like(work)
    unpack(where_ref, mine_ref, other_ref, work, pieces)
    factor_steps(low_ref, inv_ref, work, diag, dinv, left_ref, right_ref, stage, rows_ref)


def factor_steps(low_ref, inv_ref, work, diag, dinv, left_ref, right_ref, stage, rows_ref):
    width = work.shape[0]
    blocks = width // BLOCK
    left_ref[...] = jnp.zeros_like(left_ref)
    right_ref[...] = jnp.zeros_like(right_ref)

    def step(k, _):
        at = pl.multiple_of(k * BLOCK, BLOCK)
        after = pl.multiple_of(jnp.minimum(k + 1, blocks - 1) * BLOCK, BLOCK)
        diag[...] = work[pl.ds(at, BLOCK), pl.ds(at, BLOCK)]
        for i in range(blocks):
            rows = slice(i * BLOCK, (i + 1) * BLOCK)
            work[rows, :] = work[rows, :] - dot_t(left_ref[rows, :], right_ref[...])
        invert_diag(diag, dinv, stage, rows_ref)
        inverse = dinv[...]
        inv_ref[pl.ds(at, BLOCK), :] = inverse
        hi, lo = split(inverse)
        inverse = jnp.concatenate([hi, lo, hi], axis=1)
        for i in range(blocks):
            rows = slice(i * BLOCK, (i + 1) * BLOCK)
            hi, lo = split(work[rows, pl.ds(at, BLOCK)])
            new = dot_t(jnp.concatenate([hi, hi, lo], axis=1), inverse)
            new = jnp.where(i > k, new, 0.0)
            low_ref[rows, pl.ds(at, BLOCK)] = new
            hi, lo = split(new)
            left_ref[rows, :] = jnp.concatenate([hi, hi, lo], axis=1)
            right_ref[rows, :] = jnp.concatenate([hi, lo, hi], axis=1)
        ahead = right_ref[pl.ds(after, BLOCK), :]
        for i in range(blocks):
            rows = slice(i * BLOCK, (i + 1) * BLOCK)
            work[rows, pl.ds(after, BLOCK)] = work[rows, pl.ds(after, BLOCK)] - dot_t(left_ref[rows, :], ahead)
        right_ref[pl.ds(after, BLOCK), :] = jnp.zeros_like(ahead)
        return 0

    lax.fori_loop(0, blocks, step, 0)


def cholesky_parts(where, mine, other):
    count, strip, packed = mine.shape
    width = 4 * count * strip
    vmem = pl.BlockSpec(memory_space=pltpu.VMEM)
    return pl.pallas_call(
        chol_kernel,
        out_shape=(
            jax.ShapeDtypeStruct((width, width), jnp.float32),
            jax.ShapeDtypeStruct((width, BLOCK), jnp.float32),
        ),
        in_specs=[pl.BlockSpec(memory_space=pltpu.SMEM), vmem, vmem],
        out_specs=(vmem, vmem),
        scratch_shapes=[
            pltpu.VMEM((width, width), jnp.float32),
            pltpu.VMEM((2 * count, strip, packed), jnp.float32),
            pltpu.VMEM((BLOCK, BLOCK), jnp.float32),
            pltpu.VMEM((BLOCK, BLOCK), jnp.float32),
            pltpu.VMEM((width, 3 * BLOCK), jnp.bfloat16),
            pltpu.VMEM((width, 3 * BLOCK), jnp.bfloat16),
            pltpu.VMEM((8 * SUB * SUB, BLOCK), jnp.float32),
            pltpu.VMEM((BLOCK, BLOCK), jnp.float32),
        ],
        compiler_params=pltpu.CompilerParams(vmem_limit_bytes=32 << 20),
        cost_estimate=pl.CostEstimate(flops=80_000_000_000, bytes_accessed=8 << 20, transcendentals=0),
    )(where, mine, other)


def solve_kernel(gram_ref, low_ref, inv_ref, out_ref):
    _, width = gram_ref.shape
    blocks = width // BLOCK
    out_ref[...] = gram_ref[...]
    for k in range(blocks):
        cols = slice(k * BLOCK, (k + 1) * BLOCK)
        new = dot3_t(split(out_ref[:, cols]), split(inv_ref[cols, :]))
        out_ref[:, cols] = new
        if k + 1 < blocks:
            rest = slice((k + 1) * BLOCK, width)
            out_ref[:, rest] = out_ref[:, rest] - dot3_t(split(new), split(low_ref[rest, cols]))


def solve_rows(gram, low, inv):
    return pl.pallas_call(
        solve_kernel,
        out_shape=jax.ShapeDtypeStruct(gram.shape, jnp.float32),
        in_specs=[pl.BlockSpec(memory_space=pltpu.VMEM)] * 3,
        out_specs=pl.BlockSpec(memory_space=pltpu.VMEM),
        compiler_params=pltpu.CompilerParams(vmem_limit_bytes=24 << 20),
    )(gram, low, inv)


BOTH = ("obs", "unk")
OBS, UNK = 8, 16
CHIPS = UNK // 2
LINE = 4
STRIPS = 2 * LINE
WIDTH = 1024


def add_all(parts):
    total = parts[0]
    for part in parts[1:]:
        total = total + part
    return total


def swap_cores(value):
    return lax.ppermute(value, "unk", [(u, u ^ 1) for u in range(UNK)])


def over_chips(value, chips):
    got = [value]
    for k in range(1, chips):
        got.append(lax.ppermute(value, "unk", [(u, u ^ (2 * k)) for u in range(UNK)]))
    return got


def from_distance(value, k):
    return lax.ppermute(value, "obs", [(o, o ^ k) for o in range(OBS)])


def high_dot(left, right):
    return lax.dot_general(
        left, right, (((0,), (0,)), ((), ())),
        precision=lax.Precision.HIGH, preferred_element_type=jnp.float32,
    )


def local(design, weights):
    obs, unk = lax.axis_index("obs"), lax.axis_index("unk")
    chip, core = unk // 2, unk % 2
    rows = design.shape[0] // 2

    chunk = jnp.where(unk == 0, design[:, :BLOCK], 0.0)
    for j in range(1, CHIPS):
        pairs = [(o * UNK, o * UNK + 2 * j) for o in range(OBS)]
        chunk = chunk + lax.ppermute(design[:, j * BLOCK : (j + 1) * BLOCK], BOTH, pairs)

    def core_half(half):
        cut = lambda values: lax.dynamic_slice_in_dim(values, half * rows, rows, 0)
        return cut(design) * cut(weights)[:, None]

    chunk, first, second = lax.optimization_barrier((chunk, core_half(core), core_half(1 - core)))
    lower = swap_cores(chunk[rows:])
    part = jnp.where(core == 0, chunk[:rows], lower)
    mine = jnp.zeros((rows, WIDTH), jnp.float32)
    columns = over_chips(part, CHIPS)
    for k, got in enumerate(columns):
        mine = lax.dynamic_update_slice(mine, got, (0, (chip ^ k) * BLOCK))
    other = swap_cores(mine)
    first_weights = lax.dynamic_slice_in_dim(weights, core * rows, rows, 0)[:, None]
    second_weights = lax.dynamic_slice_in_dim(weights, (1 - core) * rows, rows, 0)[:, None]

    spot = chip % LINE * 2 + core

    def strips(values, scale):
        low = lax.dynamic_slice_in_dim(values, spot * STRIP, STRIP, 1)
        high = lax.dynamic_slice_in_dim(values, (2 * STRIPS - 1 - spot) * STRIP, STRIP, 1)
        return jnp.concatenate([low, high], axis=1) * scale

    strip = high_dot(strips(mine, first_weights), mine)
    partial_value = high_dot(first, mine)
    strip, partial_value, other = lax.optimization_barrier((strip, partial_value, other))
    strip = strip + high_dot(strips(other, second_weights), other)
    cut = (spot * STRIP // BLOCK + 1) * BLOCK
    high = jnp.pad(strip[STRIP:], ((0, 0), (WIDTH, BLOCK)))
    high = lax.dynamic_slice_in_dim(high, WIDTH - cut, WIDTH + BLOCK, 1)
    lanes = lax.broadcasted_iota(jnp.int32, high.shape, 1)
    piece = jnp.where(lanes < cut, jnp.pad(strip[:STRIP], ((0, 0), (0, BLOCK))), high)
    piece, partial_value, other = lax.optimization_barrier((piece, partial_value, other))
    came = from_distance(piece, 4)
    partial_value = partial_value + high_dot(second, other)
    piece, partial_value = lax.optimization_barrier((piece + came, partial_value))
    came = from_distance(piece, 1)
    owned = partial_value.shape[0] // OBS
    sends = [lax.dynamic_slice_in_dim(partial_value, (obs ^ k) * owned, owned, 0) for k in range(OBS)]
    piece, sends = lax.optimization_barrier((piece + came, sends))
    came = from_distance(piece, 2)
    piece = piece + came
    received = []
    for k in range(1, OBS):
        received.append(from_distance(sends[k], k))
    gathered = over_chips(piece, LINE)
    mine_top = jnp.stack(gathered)
    other_top = swap_cores(mine_top)
    where = jnp.stack([chip % LINE, core]).astype(jnp.int32)
    low, inverse = cholesky_parts(where, mine_top, other_top)
    owned_rows = add_all([sends[0]] + received)
    return solve_rows(owned_rows, low, inverse)


def solution(mesh):
    return jax.shard_map(
        local,
        mesh=mesh,
        in_specs=(P("obs", "unk"), P("obs")),
        out_specs=P(("unk", "obs"), None),
        check_vma=False,
    )
```

```python
import jax, jax.numpy as jnp
from jax import lax
from jax.experimental import pallas as pl
from jax.experimental.pallas import tpu as pltpu
from jax.sharding import PartitionSpec as P

BLOCK = 128
SUB = 8
STRIP = 64


def split(x):
    hi = x.astype(jnp.bfloat16)
    return hi, (x - hi.astype(jnp.float32)).astype(jnp.bfloat16)


def dot_t(a, b):
    return lax.dot_general(a, b, (((1,), (1,)), ((), ())), preferred_element_type=jnp.float32)


def dot3_t(a, b):
    (ah, al), (bh, bl) = a, b
    return dot_t(ah, bh) + (dot_t(ah, bl) + dot_t(al, bh))


def on_lanes(value, lane):
    return jnp.broadcast_to(value[:, lane : lane + 1], (SUB, BLOCK))


def invert_diag(block_ref, inv_ref, stage, rows_ref):
    lane = lax.broadcasted_iota(jnp.int32, (SUB, BLOCK), 1)
    panels = BLOCK // SUB
    groups = [block_ref[q * SUB : (q + 1) * SUB, :] for q in range(panels)]
    natural, carried = None, None
    for p in range(panels):
        r0 = p * SUB
        base = (p % 2) * 3 * SUB * SUB
        one = lambda row: stage[pl.ds(base + row, SUB, stride=0), :]
        panel = groups[p]
        columns = [on_lanes(panel, r0 + c) for c in range(SUB)]
        if natural is not None:
            for i in range(SUB):
                stage[base + i * SUB : base + (i + 1) * SUB, :] = on_lanes(natural, r0 + i)
            panel = jnp.where((lane >= r0 - SUB) & (lane < r0), 0.0, panel)
            for k in range(SUB):
                down = stage[pl.ds(base + k, SUB, stride=SUB), :]
                panel = panel - down * carried[k]
                for c in range(SUB):
                    columns[c] = columns[c] - down * one(c * SUB + k)
        inside = (lane >= r0) & (lane < r0 + SUB)
        sub = lax.broadcasted_iota(jnp.int32, (SUB, BLOCK), 0)
        panel = jnp.where(inside, jnp.where(lane == r0 + sub, 1.0, 0.0), panel)
        at = SUB * SUB
        for c in range(SUB):
            stage[base + at + c * SUB : base + at + (c + 1) * SUB, :] = columns[c]
        stage[base + 2 * at : base + 2 * at + SUB, :] = panel
        e = {(i, c): one(at + c * SUB + i) for c in range(SUB) for i in range(c + 1)}
        w = [one(2 * at + i) for i in range(SUB)]
        for c in range(SUB):
            inv = lax.rsqrt(e[c, c])
            w[c] = w[c] * inv
            u = {i: e[c, i] * inv for i in range(c + 1, SUB)}
            for i in range(c + 1, SUB):
                w[i] = w[i] - u[i] * w[c]
                for j in range(i, SUB):
                    e[i, j] = e[i, j] - u[i] * u[j]
            rows_ref[r0 + c : r0 + c + 1, :] = w[c][0:1, :]
        natural, carried = rows_ref[r0 : r0 + SUB, :], w
        inv_ref[r0 : r0 + SUB, :] = jnp.where(lane < r0 + SUB, natural, 0.0)
        if p + 2 < panels:
            for q in range(p + 2, panels):
                spare = 6 * SUB * SUB + (q % 2) * SUB * SUB
                for i in range(SUB):
                    stage[spare + i * SUB : spare + (i + 1) * SUB, :] = on_lanes(natural, q * SUB + i)
                groups[q] = jnp.where(inside, 0.0, groups[q])
                for k in range(SUB):
                    groups[q] = groups[q] - stage[pl.ds(spare + k, SUB, stride=SUB), :] * w[k]


def unpack(where_ref, mine_ref, other_ref, work, pieces):
    count = mine_ref.shape[0]
    chip, core = where_ref[0], where_ref[1]
    for k in range(count):
        pieces[2 * (chip ^ k) + core] = mine_ref[k]
        pieces[2 * (chip ^ k) + 1 - core] = other_ref[k]
    for t in range(2 * count):
        low, high = t * STRIP, (4 * count - 1 - t) * STRIP
        cut, rest = (low // BLOCK + 1) * BLOCK, (high // BLOCK + 1) * BLOCK
        work[low : low + STRIP, :cut] = pieces[t, :, :cut]
        work[high : high + STRIP, :rest] = pieces[t, :, cut:]


def chol_kernel(where_ref, mine_ref, other_ref, low_ref, inv_ref, work, pieces, diag, dinv, left_ref, right_ref, stage, rows_ref):
    work[...] = jnp.zeros_like(work)
    unpack(where_ref, mine_ref, other_ref, work, pieces)
    factor_steps(low_ref, inv_ref, work, diag, dinv, left_ref, right_ref, stage, rows_ref)


def factor_steps(low_ref, inv_ref, work, diag, dinv, left_ref, right_ref, stage, rows_ref):
    width = work.shape[0]
    blocks = width // BLOCK
    left_ref[...] = jnp.zeros_like(left_ref)
    right_ref[...] = jnp.zeros_like(right_ref)

    def step(k, _):
        at = pl.multiple_of(k * BLOCK, BLOCK)
        after = pl.multiple_of(jnp.minimum(k + 1, blocks - 1) * BLOCK, BLOCK)
        diag[...] = work[pl.ds(at, BLOCK), pl.ds(at, BLOCK)]
        for i in range(blocks):
            rows = slice(i * BLOCK, (i + 1) * BLOCK)
            work[rows, :] = work[rows, :] - dot_t(left_ref[rows, :], right_ref[...])
        invert_diag(diag, dinv, stage, rows_ref)
        inverse = dinv[...]
        inv_ref[pl.ds(at, BLOCK), :] = inverse
        hi, lo = split(inverse)
        inverse = jnp.concatenate([hi, lo, hi], axis=1)
        for i in range(blocks):
            rows = slice(i * BLOCK, (i + 1) * BLOCK)
            hi, lo = split(work[rows, pl.ds(at, BLOCK)])
            new = dot_t(jnp.concatenate([hi, hi, lo], axis=1), inverse)
            new = jnp.where(i > k, new, 0.0)
            low_ref[rows, pl.ds(at, BLOCK)] = new
            hi, lo = split(new)
            left_ref[rows, :] = jnp.concatenate([hi, hi, lo], axis=1)
            right_ref[rows, :] = jnp.concatenate([hi, lo, hi], axis=1)
        ahead = right_ref[pl.ds(after, BLOCK), :]
        for i in range(blocks):
            rows = slice(i * BLOCK, (i + 1) * BLOCK)
            work[rows, pl.ds(after, BLOCK)] = work[rows, pl.ds(after, BLOCK)] - dot_t(left_ref[rows, :], ahead)
        right_ref[pl.ds(after, BLOCK), :] = jnp.zeros_like(ahead)
        return 0

    lax.fori_loop(0, blocks, step, 0)


def cholesky_parts(where, mine, other):
    count, strip, packed = mine.shape
    width = 4 * count * strip
    vmem = pl.BlockSpec(memory_space=pltpu.VMEM)
    return pl.pallas_call(
        chol_kernel,
        out_shape=(
            jax.ShapeDtypeStruct((width, width), jnp.float32),
            jax.ShapeDtypeStruct((width, BLOCK), jnp.float32),
        ),
        in_specs=[pl.BlockSpec(memory_space=pltpu.SMEM), vmem, vmem],
        out_specs=(vmem, vmem),
        scratch_shapes=[
            pltpu.VMEM((width, width), jnp.float32),
            pltpu.VMEM((2 * count, strip, packed), jnp.float32),
            pltpu.VMEM((BLOCK, BLOCK), jnp.float32),
            pltpu.VMEM((BLOCK, BLOCK), jnp.float32),
            pltpu.VMEM((width, 3 * BLOCK), jnp.bfloat16),
            pltpu.VMEM((width, 3 * BLOCK), jnp.bfloat16),
            pltpu.VMEM((8 * SUB * SUB, BLOCK), jnp.float32),
            pltpu.VMEM((BLOCK, BLOCK), jnp.float32),
        ],
        compiler_params=pltpu.CompilerParams(vmem_limit_bytes=32 << 20),
        cost_estimate=pl.CostEstimate(flops=80_000_000_000, bytes_accessed=8 << 20, transcendentals=0),
    )(where, mine, other)


def solve_kernel(gram_ref, low_ref, inv_ref, out_ref):
    _, width = gram_ref.shape
    blocks = width // BLOCK
    out_ref[...] = gram_ref[...]
    for k in range(blocks):
        cols = slice(k * BLOCK, (k + 1) * BLOCK)
        new = dot3_t(split(out_ref[:, cols]), split(inv_ref[cols, :]))
        out_ref[:, cols] = new
        if k + 1 < blocks:
            rest = slice((k + 1) * BLOCK, width)
            out_ref[:, rest] = out_ref[:, rest] - dot3_t(split(new), split(low_ref[rest, cols]))


def solve_rows(gram, low, inv):
    return pl.pallas_call(
        solve_kernel,
        out_shape=jax.ShapeDtypeStruct(gram.shape, jnp.float32),
        in_specs=[pl.BlockSpec(memory_space=pltpu.VMEM)] * 3,
        out_specs=pl.BlockSpec(memory_space=pltpu.VMEM),
        compiler_params=pltpu.CompilerParams(vmem_limit_bytes=24 << 20),
    )(gram, low, inv)


BOTH = ("obs", "unk")
OBS, UNK = 8, 16
CHIPS = UNK // 2
LINE = 4
STRIPS = 2 * LINE
WIDTH = 1024


def add_all(parts):
    total = parts[0]
    for part in parts[1:]:
        total = total + part
    return total


def swap_cores(value):
    return lax.ppermute(value, "unk", [(u, u ^ 1) for u in range(UNK)])


def over_chips(value, chips):
    return [value] + [
        lax.ppermute(value, "unk", [(u, u ^ (2 * k)) for u in range(UNK)]) for k in range(1, chips)
    ]


def from_distance(value, k):
    return lax.ppermute(value, "obs", [(o, o ^ k) for o in range(OBS)])


def high_dot(left, right):
    return lax.dot_general(
        left, right, (((0,), (0,)), ((), ())),
        precision=lax.Precision.HIGH, preferred_element_type=jnp.float32,
    )


def local(design, weights):
    obs, unk = lax.axis_index("obs"), lax.axis_index("unk")
    chip, core = unk // 2, unk % 2
    rows = design.shape[0] // 2

    chunk = jnp.where(unk == 0, design[:, :BLOCK], 0.0)
    for j in range(1, CHIPS):
        pairs = [(o * UNK, o * UNK + 2 * j) for o in range(OBS)]
        chunk = chunk + lax.ppermute(design[:, j * BLOCK : (j + 1) * BLOCK], BOTH, pairs)

    def core_half(half):
        cut = lambda values: lax.dynamic_slice_in_dim(values, half * rows, rows, 0)
        return cut(design) * cut(weights)[:, None]

    chunk, first, second = lax.optimization_barrier((chunk, core_half(core), core_half(1 - core)))
    lower = swap_cores(chunk[rows:])
    part = jnp.where(core == 0, chunk[:rows], lower)
    mine = jnp.zeros((rows, WIDTH), jnp.float32)
    for k, got in enumerate(over_chips(part, CHIPS)):
        mine = lax.dynamic_update_slice(mine, got, (0, (chip ^ k) * BLOCK))
    other = swap_cores(mine)
    first_weights = lax.dynamic_slice_in_dim(weights, core * rows, rows, 0)[:, None]
    second_weights = lax.dynamic_slice_in_dim(weights, (1 - core) * rows, rows, 0)[:, None]

    spot = chip % LINE * 2 + core

    def strips(values, scale):
        low = lax.dynamic_slice_in_dim(values, spot * STRIP, STRIP, 1)
        high = lax.dynamic_slice_in_dim(values, (2 * STRIPS - 1 - spot) * STRIP, STRIP, 1)
        return jnp.concatenate([low, high], axis=1) * scale

    strip = high_dot(strips(mine, first_weights), mine)
    strip, other = lax.optimization_barrier((strip, other))
    strip = strip + high_dot(strips(other, second_weights), other)
    cut = (spot * STRIP // BLOCK + 1) * BLOCK
    high = jnp.pad(strip[STRIP:], ((0, 0), (WIDTH, BLOCK)))
    high = lax.dynamic_slice_in_dim(high, WIDTH - cut, WIDTH + BLOCK, 1)
    lanes = lax.broadcasted_iota(jnp.int32, high.shape, 1)
    piece = jnp.where(lanes < cut, jnp.pad(strip[:STRIP], ((0, 0), (0, BLOCK))), high)
    piece, mine, other = lax.optimization_barrier((piece, mine, other))
    came = from_distance(piece, 4)
    partial_value = high_dot(first, mine)
    piece, partial_value, other = lax.optimization_barrier((piece + came, partial_value, other))
    came = from_distance(piece, 1)
    partial_value = partial_value + high_dot(second, other)
    owned = partial_value.shape[0] // OBS
    sends = [lax.dynamic_slice_in_dim(partial_value, (obs ^ k) * owned, owned, 0) for k in range(OBS)]
    piece, sends = lax.optimization_barrier((piece + came, sends))
    came = from_distance(piece, 2)
    piece = piece + came
    received = []
    for k in range(1, OBS):
        received.append(from_distance(sends[k], k))
    gathered = over_chips(piece, LINE)
    mine_top = jnp.stack(gathered)
    other_top = swap_cores(mine_top)
    where = jnp.stack([chip % LINE, core]).astype(jnp.int32)
    low, inverse = cholesky_parts(where, mine_top, other_top)
    owned_rows = add_all([sends[0]] + received)
    return solve_rows(owned_rows, low, inverse)


def solution(mesh):
    return jax.shard_map(
        local,
        mesh=mesh,
        in_specs=(P("obs", "unk"), P("obs")),
        out_specs=P(("unk", "obs"), None),
        check_vma=False,
    )
```
